32 devices in a mesh: pipe: 8 (over y, x, core), tensor: 4 (over z).
Axes of the slice: x: 2, y: 2, z: 4, core: 2. Of those that a mesh axis runs over, the one named last changes fastest.
Arguments:
- fwd_inputs: bfloat16 [8, 576, 1536], P('pipe'), may hold values from -6 to 6
- bwd_inputs: bfloat16 [8, 576, 1536], P('pipe'), may hold values from -6 to 6
- bwd_cotangent: bfloat16 [8, 576, 1536], P('pipe'), may hold values from -6 to 6
- fwd_lengths: int32 [8, 8], P('pipe'), may hold values from 1 to 192, 576 in all within a row
- bwd_lengths: int32 [8, 8], P('pipe'), may hold values from 1 to 192, 576 in all within a row
- norm_gains: bfloat16 [2, 8, 1536], P(None, 'pipe'), may hold values from 0.25 to 1.75
- query_weight: bfloat16 [2, 8, 1536, 1536], P(None, 'pipe', None, 'tensor'), may hold values from -1 to 1
- key_weight: bfloat16 [2, 8, 1536, 1536], P(None, 'pipe', None, 'tensor'), may hold values from -1 to 1
- value_weight: bfloat16 [2, 8, 1536, 1536], P(None, 'pipe', None, 'tensor'), may hold values from -0.15625 to 0.15625
- out_weight: bfloat16 [2, 8, 1536, 1536], P(None, 'pipe', 'tensor'), may hold values from -0.15625 to 0.15625
Outputs:
- next_inputs: bfloat16 [8, 576, 1536], P('pipe', 'tensor')
- next_cotangent: bfloat16 [8, 576, 1536], P('pipe', 'tensor')
- out_weight_grad: float32 [8, 1536, 1536], P('pipe', 'tensor')
The draws below stay inside these ranges and needn't reach their ends.
Inputs may be any that keep to these rules, and one draw needn't show every extreme that they name: `fwd_lengths`: each microbatch's mesh lengths sum to 576; the longest is exactly 192. `bwd_lengths`: each microbatch's mesh lengths sum to 576; the longest is exactly 192.
All inputs are finite; a program needn't handle non-finite values.
Results may differ from the reference program's by a relative error of at most 0.019.
Values may be sent and summed in bfloat16 or wider, within the bound.
A program may use at most 64 MiB of HBM per device.

```python
import math
import jax
import jax.numpy as jnp
import numpy as np
from jax import lax

D = 1536
HEADS = 12
HEAD_DIM = 128
ROWS = 576
DOCS = 8
MOST = 192
SECTIONS = 8
N_TENSOR = 4


def own_normal(key, salt):
    return jnp.clip(jax.random.normal(jax.random.fold_in(key, salt), (2, SECTIONS, D, HEADS * HEAD_DIM), jnp.float32), -5.0, 5.0)


def projection_draw(key, salt):
    own = own_normal(key, salt)
    result = own * D ** (-0.5)
    return jnp.clip(result, -1.0, 1.0).astype(jnp.bfloat16)


def draw_query_weight(key, part):
    return projection_draw(key, 202)


def draw_key_weight(key, part):
    return projection_draw(key, 303)


def shard_levels(stream_key, dims, pieces, low, largest):
    loudness, own = 1.0, jax.random.fold_in(stream_key, 6)
    for axis_at, blocks in pieces:
        heights = jnp.exp(jax.random.uniform(jax.random.fold_in(own, axis_at), (blocks,), jnp.float32, low / len(pieces), largest / len(pieces)))
        loudness = loudness * jnp.repeat(heights, dims[axis_at] // blocks).reshape([-1 if axis == axis_at else 1 for axis in range(len(dims))])
    return loudness


def profile(amount, total, bound, lean):
    weights = [(1 << 20) // math.isqrt(standing ** lean) + 1 for standing in range(2, amount + 1)]
    surplus, given = total - bound - (amount - 1), [1] * (amount - 1)
    while surplus > 0:
        free = [i for i in range(amount - 1) if given[i] < bound]
        whole, left = sum([weights[i] for i in free]), surplus
        for i in free:
            addition = min(bound - given[i], max(1, left * weights[i] // whole), surplus)
            given[i] = given[i] + addition
            surplus = surplus - addition
    return np.array([bound] + given)


def uneven(stream_key, amount, total, reach, lean):
    if amount == 2:
        one = jax.random.randint(stream_key, (), max(1, total - reach), min(reach, total - 1) + 1)
        return jnp.stack([one, total - one])
    tallies = jnp.asarray(profile(amount, total, reach, lean), jnp.int32)
    pairs = (amount - 1) // 2
    giver, sink = tallies[1:1 + 2 * pairs:2], tallies[2:2 + 2 * pairs:2]
    slack = jnp.minimum(giver - 1, reach - sink)
    shifted = jax.random.randint(jax.random.fold_in(stream_key, 1), (pairs,), 0, 1 << 20) % (slack + 1)
    tallies = tallies.at[1:1 + 2 * pairs:2].set(giver - shifted).at[2:2 + 2 * pairs:2].set(sink + shifted)
    return tallies[jax.random.permutation(jax.random.fold_in(stream_key, 2), amount)]


def normal_values(rng, extent, deviation, bound, pieces=(), kind=jnp.bfloat16):
    values = deviation * jax.random.normal(rng, extent, jnp.float32)
    if pieces:
        values = values * shard_levels(rng, extent, pieces, -0.22, 0.18)
    return jnp.clip(values, -bound, bound).astype(kind)


def setup_inputs(seed: int = 0) -> dict:
    key_of = jax.random.split(jax.random.key(seed), 11)
    return {
        "fwd_inputs": normal_values(key_of[0], (SECTIONS, ROWS, D), 1.0, 6.0, ((0, 8),)),
        "bwd_inputs": normal_values(key_of[1], (SECTIONS, ROWS, D), 1.0, 6.0, ((0, 8),)),
        "bwd_cotangent": normal_values(key_of[2], (SECTIONS, ROWS, D), 1.0, 6.0, ((0, 8),)),
        "fwd_lengths": jax.vmap(lambda own: uneven(own, DOCS, ROWS, MOST, 2))(jax.random.split(key_of[3], SECTIONS)).reshape((SECTIONS, DOCS)).astype(jnp.int32),
        "bwd_lengths": jax.vmap(lambda own: uneven(own, DOCS, ROWS, MOST, 2))(jax.random.split(key_of[4], SECTIONS)).reshape((SECTIONS, DOCS)).astype(jnp.int32),
        "norm_gains": jnp.clip(1.0 + 0.15 * jax.random.normal(key_of[5], (2, SECTIONS, D), jnp.float32), 0.25, 1.75).astype(jnp.bfloat16),
        "query_weight": draw_query_weight(jax.random.fold_in(key_of[10], 71), 0),
        "key_weight": draw_key_weight(jax.random.fold_in(key_of[10], 71), 0),
        "value_weight": normal_values(key_of[8], (2, SECTIONS, D, HEADS * HEAD_DIM), D ** -0.5, 0.15625, ((1, 8), (3, 4))),
        "out_weight": normal_values(key_of[9], (2, SECTIONS, HEADS * HEAD_DIM, D), (HEADS * HEAD_DIM) ** -0.5, 0.15625, ((1, 8), (2, 4))),
    }


def rms_norm(activation, gain_vec):
    widened = activation.astype(jnp.float32)
    mean_square = lax.optimization_barrier(jnp.mean(widened * widened, axis=-1, keepdims=True))
    return (widened * lax.rsqrt(mean_square + 1e-05) * gain_vec.astype(jnp.float32)).astype(jnp.bfloat16)

def doc_mask(lengths, row_count):
    doc_ends = jnp.cumsum(lengths).astype(jnp.int32)
    position = jnp.arange(row_count, dtype=jnp.int32)
    segment = lax.optimization_barrier(jnp.sum((position[:, None] >= doc_ends[None, :]).astype(jnp.int32), axis=1))
    return (segment[:, None] == segment[None, :]) & (position[None, :] <= position[:, None])

def head_block(normed, w_query, w_key, w_value, w_out, keep_mask):
    row_count = normed.shape[0]
    group_count = w_query.shape[1] // HEAD_DIM

    def project(weight):
        return jnp.dot(normed, weight, preferred_element_type=jnp.float32).astype(jnp.bfloat16).reshape(row_count, group_count, HEAD_DIM)
    queries = project(w_query)
    key_rows = project(w_key)
    value_rows = project(w_value)
    scores = jnp.einsum('qgh,kgh->gqk', queries.astype(jnp.float32), key_rows.astype(jnp.float32)) * HEAD_DIM ** (-0.5)
    scores = jnp.where(keep_mask[None], scores, -1e+30)
    row_max = lax.optimization_barrier(jnp.max(scores, axis=-1, keepdims=True))
    weights = jnp.where(keep_mask[None], jnp.exp(scores - row_max), 0.0)
    weights_bf = (weights / lax.optimization_barrier(jnp.sum(weights, axis=-1, keepdims=True))).astype(jnp.bfloat16)
    attended = jnp.einsum('gqk,kgh->qgh', weights_bf.astype(jnp.float32), value_rows.astype(jnp.float32)).astype(jnp.bfloat16)
    attended = attended.reshape(row_count, group_count * HEAD_DIM)
    return (jnp.dot(attended, w_out, preferred_element_type=jnp.float32), attended)

def section_forward(inputs, gain_vec, w_query, w_key, w_value, w_out, lengths):
    keep_mask = doc_mask(lengths, inputs.shape[0])
    normed = rms_norm(inputs, gain_vec)
    group_width = w_query.shape[1] // N_TENSOR
    total = jnp.zeros(inputs.shape, jnp.float32)
    for member in range(N_TENSOR):
        column_span = slice(member * group_width, (member + 1) * group_width)
        partial_out, unused = head_block(normed, w_query[:, column_span], w_key[:, column_span], w_value[:, column_span], w_out[column_span, :], keep_mask)
        rounded = lax.optimization_barrier(partial_out.astype(jnp.bfloat16))
        total = total + rounded.astype(jnp.float32)
    return (inputs.astype(jnp.float32) + total).astype(jnp.bfloat16)

def section_backward(inputs, cotangent, gain_vec, w_query, w_key, w_value, w_out, lengths):
    keep_mask = doc_mask(lengths, inputs.shape[0])
    group_width = w_query.shape[1] // N_TENSOR
    total = jnp.zeros(inputs.shape, jnp.float32)
    grad_parts = []
    for member in range(N_TENSOR):
        column_span = slice(member * group_width, (member + 1) * group_width)

        def branch(activation):
            return head_block(rms_norm(activation, gain_vec), w_query[:, column_span], w_key[:, column_span], w_value[:, column_span], w_out[column_span, :], keep_mask)
        unused, pull_back, attended = jax.vjp(branch, inputs, has_aux=True)
        input_grad, = pull_back(cotangent.astype(jnp.float32))
        total = total + input_grad.astype(jnp.float32)
        grad_parts.append(lax.dot_general(attended, cotangent, (((0,), (0,)), ((), ())), preferred_element_type=jnp.float32))
    return ((cotangent.astype(jnp.float32) + total).astype(jnp.bfloat16), jnp.concatenate(grad_parts, axis=0))

def reference(fwd_inputs, bwd_inputs, bwd_cotangent, fwd_lengths, bwd_lengths, norm_gains, query_weight, key_weight, value_weight, out_weight):

    def per_section(bundle):
        fin, bin_, bcot, flen, blen, gain_f, gain_b, wq_f, wq_b, wk_f, wk_b, wv_f, wv_b, wo_f, wo_b = bundle
        section_out = section_forward(fin, gain_f, wq_f, wk_f, wv_f, wo_f, flen)
        input_cot, grad_mirror = section_backward(bin_, bcot, gain_b, wq_b, wk_b, wv_b, wo_b, blen)
        return (section_out, input_cot, grad_mirror)
    section_outs, input_cots, grad_mirrors = lax.map(per_section, (fwd_inputs, bwd_inputs, bwd_cotangent, fwd_lengths, bwd_lengths, norm_gains[0], norm_gains[1], query_weight[0], query_weight[1], key_weight[0], key_weight[1], value_weight[0], value_weight[1], out_weight[0], out_weight[1]))
    zero_block = jnp.zeros((1,) + section_outs.shape[1:], jnp.bfloat16)
    next_inputs = jnp.concatenate([zero_block, section_outs[:-1]], axis=0)
    next_cotangent = jnp.concatenate([zero_block, input_cots[:-1]], axis=0)
    out_weight_grad = jnp.flip(grad_mirrors, axis=0)
    return (next_inputs, next_cotangent, out_weight_grad)
```

```python
import functools

import jax
import jax.numpy as jnp
from jax import lax
from jax.experimental import pallas as pl
from jax.experimental.pallas import tpu as pltpu
from jax.sharding import PartitionSpec as P

HEAD_DIM = 128
MOST = 192
VMEM_LIMIT = 60 * 1024 * 1024
MESH = pl.DeviceIdType.MESH
RIGHT, LEFT = 0, 1
FWD, BWD = 0, 1
F32 = jnp.float32
BF16 = jnp.bfloat16


def doc_start(lengths_ref, first_row, row_count):
    position = lax.broadcasted_iota(jnp.int32, (row_count, 1), 0) + first_row
    start = jnp.zeros((row_count, 1), jnp.int32)
    end = jnp.int32(0)
    for doc in range(lengths_ref.shape[1]):
        end = end + lengths_ref[0, doc]
        start = jnp.where(position >= end, end, start)
    return position, start


def window_mask(lengths_ref, first_row, row_count, first_key, key_count):
    position, start = doc_start(lengths_ref, first_row, row_count)
    keys = lax.broadcasted_iota(jnp.int32, (row_count, key_count), 1) + first_key
    return (keys >= start) & (keys <= position)


def dot_nn(left, right):
    return jnp.dot(left, right, preferred_element_type=F32)


def dot_nt(left, right):
    return lax.dot_general(left, right, (((1,), (1,)), ((), ())), preferred_element_type=F32)


def dot_tn(left, right):
    return lax.dot_general(left, right, (((0,), (0,)), ((), ())), preferred_element_type=F32)


def normed_rows(x, gain):
    widened = x.astype(F32)
    mean_square = jnp.mean(widened * widened, axis=-1, keepdims=True)
    scale = lax.rsqrt(mean_square + 1e-05)
    return (widened * scale * gain).astype(BF16), scale


def score_block(queries, key_rows, keep):
    scores = dot_nt(queries, key_rows) * HEAD_DIM ** (-0.5)
    scores = jnp.where(keep, scores, -1e30)
    weights = jnp.exp(scores - jnp.max(scores, axis=-1, keepdims=True))
    return weights, 1.0 / jnp.sum(weights, axis=-1, keepdims=True)


def rows_at(first, count):
    return pl.ds(pl.multiple_of(first, 16), count)


def sections_kernel(
    pipes, peers, pieces,
    len_f_hbm, len_b_hbm, gain_hbm, xf_hbm, xb_hbm, c_hbm, wq_hbm, wk_hbm, wv_hbm, wo_hbm,
    outf_ref, outb_ref, grad_ref,
    lens_f, lens_b, gain_ref, xf, xb, c_ref, wf, wb, wof, wob, qkvf, qkvb, dqkv, att,
    termf, termb, own, grad_out, mid_recv, last_recv, own_recv,
    load_sem, chain_send, chain_recv, own_send_sem, own_recv_sem, grad_sems,
):
    p = lax.axis_index("pipe")
    t = lax.axis_index("tensor")
    rows, wide = xf.shape
    width = wof.shape[0]
    heads = width // HEAD_DIM
    share = rows // peers
    piece = share // pieces
    blocks = rows // MOST
    last = peers - 1
    sends = p < pipes - 1
    takes = p > 0
    terms = (termf, termb)
    inputs = (xf, c_ref)

    slot = iter(range(load_sem.shape[0]))

    def load(source, target):
        copy = pltpu.make_async_copy(source, target, load_sem.at[next(slot)])
        copy.start()
        return copy

    low_half = t < peers // 2
    order = [jnp.where(low_half, blocks - 1 - i, i) for i in range(blocks)]

    lens_f_copy = load(len_f_hbm, lens_f)
    gain_copy = load(gain_hbm, gain_ref)
    x_copies = [
        load(xf_hbm.at[0, rows_at(b * MOST, MOST)], xf.at[rows_at(b * MOST, MOST)]) for b in order
    ]
    wf_copies = [
        load(source.at[0, 0], wf.at[:, part * width : (part + 1) * width])
        for part, source in enumerate((wq_hbm, wk_hbm, wv_hbm))
    ]
    wof_copy = load(wo_hbm.at[0, 0], wof)

    barrier = pltpu.get_barrier_semaphore()
    to_right, to_left = t < last, t > 0
    roles = [
        (sends & to_right, sends & to_left, (p, t - 1)),
        (sends & to_left, sends & to_right, (p, t + 1)),
        (sends, takes, (p - 1, t)),
        (sends & to_right, takes & to_left, (p - 1, t - 1)),
        (sends & to_left, takes & to_right, (p - 1, t + 1)),
        (None, None, (pipes - 1 - p, t)),
    ]

    def when(condition):
        if condition is None:
            return lambda body: body()
        return pl.when(condition)

    for unused, has_source, source in roles:

        @when(has_source)
        def greet():
            pl.semaphore_signal(barrier, inc=1, device_id=source, device_id_type=MESH)

    def await_barrier():
        count = jnp.int32(0)
        for has_target, unused, unused_too in roles:
            count = count + (1 if has_target is None else has_target.astype(jnp.int32))
        pl.semaphore_wait(barrier, count)

    places = (t, last - t)

    def owner_at(flow, step):
        owner = peers - step + places[flow]
        return owner if flow == RIGHT else last - owner

    def chain_copies(flow, way, step, owner, only=None):
        toward = t + 1 if flow == RIGHT else t - 1
        copies = []
        count = pieces if step == last else 1
        size = share // count
        for part in range(count) if only is None else [only]:
            if step == last:
                target = last_recv.at[flow, way, part * size : (part + 1) * size]
                device = (p + 1, toward)
            else:
                target = mid_recv.at[flow, way, step - 1]
                device = (p, toward)
            copies.append(
                pltpu.make_async_remote_copy(
                    src_ref=terms[way].at[rows_at(owner * share + part * size, size)],
                    dst_ref=target,
                    send_sem=chain_send.at[flow, way, step - 1, part],
                    recv_sem=chain_recv.at[flow, way, step - 1, part],
                    device_id=device,
                    device_id_type=MESH,
                )
            )
        return copies

    def start_edges(way, steps):
        for flow in (RIGHT, LEFT):

            @pl.when(sends & (places[flow] == 0))
            def start():
                for step in steps:
                    owner = peers - step if flow == RIGHT else step - 1
                    for copy in chain_copies(flow, way, step, owner):
                        copy.start()

    def pass_on(way, step):
        for flow in (RIGHT, LEFT):
            here = places[flow]

            @pl.when(sends & (here >= 1) & (here < step))
            def add():
                owner = owner_at(flow, step)
                for copy in chain_copies(flow, way, step - 1, owner):
                    copy.wait_recv()
                for part in range(pieces):
                    at = rows_at(owner * share + part * piece, piece)
                    arrived = mid_recv[flow, way, step - 2, part * piece : (part + 1) * piece, :]
                    total = terms[way][at, :].astype(F32) + arrived.astype(F32)
                    terms[way][at, :] = total.astype(BF16)
                for copy in chain_copies(flow, way, step, owner):
                    copy.start()

    def own_copy(way):
        return pltpu.make_async_remote_copy(
            src_ref=own.at[way],
            dst_ref=own_recv.at[way],
            send_sem=own_send_sem.at[way],
            recv_sem=own_recv_sem.at[way],
            device_id=(p + 1, t),
            device_id_type=MESH,
        )

    def send_own(way):
        @pl.when(sends)
        def send():
            at = rows_at(t * share, share)
            total = inputs[way][at, :].astype(F32) + terms[way][at, :].astype(F32)
            own[way] = total.astype(BF16)
            own_copy(way).start()

    def finish(way, out_ref):
        @pl.when(takes)
        def receive():
            own_copy(way).wait_recv()

        for part in range(pieces):
            at = slice(part * piece, (part + 1) * piece)
            for flow in (RIGHT, LEFT):

                @pl.when(takes & (places[flow] >= 1))
                def arrive():
                    chain_copies(flow, way, last, t, part)[0].wait_recv()

            total = own_recv[way, at, :].astype(F32) + last_recv[RIGHT, way, at, :].astype(F32)
            total = total + last_recv[LEFT, way, at, :].astype(F32)
            out_ref[at, :] = total.astype(BF16)

    zeros = jnp.zeros((share, wide), BF16)

    @pl.when(jnp.logical_not(takes))
    def clear_own():
        for way in (FWD, BWD):
            own_recv[way] = zeros

    for flow in (RIGHT, LEFT):

        @pl.when(jnp.logical_not(takes) | (places[flow] == 0))
        def clear_last():
            for way in (FWD, BWD):
                last_recv[flow, way] = zeros

    qkvf[0:MOST, :] = jnp.zeros((MOST, 3 * width), BF16)
    gain_copy.wait()
    gain_f = gain_ref[0:1, :].astype(F32)
    gain_b = gain_ref[1:2, :].astype(F32)

    def project_forward(i):
        x_copies[i].wait()
        normed, unused = normed_rows(xf[rows_at(order[i] * MOST, MOST), :], gain_f)
        if i == 0:
            for copy in wf_copies:
                copy.wait()
        qkvf[rows_at((order[i] + 1) * MOST, MOST), :] = dot_nn(normed, wf[...]).astype(BF16)

    def attend_forward(i):
        low = order[i] * MOST
        query_at = rows_at(low + MOST, MOST)
        key_at = rows_at(low, 2 * MOST)
        keep = window_mask(lens_f, low, MOST, low - MOST, 2 * MOST)
        parts = []
        for head in range(heads):
            at = head * HEAD_DIM
            weights, inverse = score_block(
                qkvf[query_at, at : at + HEAD_DIM],
                qkvf[key_at, width + at : width + at + HEAD_DIM],
                keep,
            )
            mixed = dot_nn(
                (weights * inverse).astype(BF16),
                qkvf[key_at, 2 * width + at : 2 * width + at + HEAD_DIM],
            )
            parts.append(mixed.astype(BF16))
        attended = jnp.concatenate(parts, axis=1)
        if i == 0:
            wof_copy.wait()
        termf[rows_at(low, MOST), :] = dot_nn(attended, wof[...]).astype(BF16)

    project_forward(0)
    project_forward(1)
    xb_copy = load(xb_hbm.at[0], xb)
    wb_copies = [
        load(source.at[1, 0], wb.at[:, part * width : (part + 1) * width])
        for part, source in enumerate((wq_hbm, wk_hbm, wv_hbm))
    ]
    c_copy = load(c_hbm.at[0], c_ref)
    wob_copy = load(wo_hbm.at[1, 0], wob)
    lens_b_copy = load(len_b_hbm, lens_b)
    lens_f_copy.wait()
    attend_forward(0)
    await_barrier()
    start_edges(FWD, [1])
    project_forward(2)
    attend_forward(1)
    attend_forward(2)
    start_edges(FWD, range(2, peers))
    send_own(FWD)

    xb_copy.wait()
    scales = []
    for block in range(blocks):
        low, high = block * MOST, (block + 1) * MOST
        normed, scale = normed_rows(xb[low:high, :], gain_b)
        scales.append(scale)
        if block == 0:
            for copy in wb_copies:
                copy.wait()
        qkvb[low:high, :] = dot_nn(normed, wb[...]).astype(BF16)
    c_copy.wait()
    wob_copy.wait()
    lens_b_copy.wait()
    middle = [step for step in range(2, peers)]
    pass_on(FWD, middle[0])
    carried = {}
    for block in range(blocks):
        low, high = block * MOST, (block + 1) * MOST
        key_low = max(0, low - MOST)
        keep = window_mask(lens_b, low, MOST, key_low, high - key_low)
        d_attended = dot_nt(c_ref[low:high, :], wob[...]).astype(BF16)
        for head in range(heads):
            at = head * HEAD_DIM
            cols = [slice(part * width + at, part * width + at + HEAD_DIM) for part in range(3)]
            queries = qkvb[low:high, cols[0]]
            key_rows = qkvb[key_low:high, cols[1]]
            value_rows = qkvb[key_low:high, cols[2]]
            weights, inverse = score_block(queries, key_rows, keep)
            probs = weights * inverse
            probs_bf = probs.astype(BF16)
            mixed = dot_nn(probs_bf, value_rows)
            att[low:high, at : at + HEAD_DIM] = mixed.astype(BF16)
            d_mixed = d_attended[:, at : at + HEAD_DIM]
            d_probs = dot_nt(d_mixed, value_rows)
            delta = jnp.sum(mixed * d_mixed.astype(F32), axis=-1, keepdims=True)
            d_scores = (probs * (d_probs - delta) * HEAD_DIM ** (-0.5)).astype(BF16)
            dqkv[low:high, cols[0]] = dot_nn(d_scores, key_rows).astype(BF16)
            d_keys = dot_tn(d_scores, queries)
            d_values = dot_tn(probs_bf, d_mixed)
            if block > 0:
                past_keys, past_values = carried[head]
                dqkv[key_low:low, cols[1]] = (past_keys + d_keys[:MOST]).astype(BF16)
                dqkv[key_low:low, cols[2]] = (past_values + d_values[:MOST]).astype(BF16)
                d_keys, d_values = d_keys[MOST:], d_values[MOST:]
            if block == blocks - 1:
                dqkv[low:high, cols[1]] = d_keys.astype(BF16)
                dqkv[low:high, cols[2]] = d_values.astype(BF16)
            carried[head] = (d_keys, d_values)
    for block in range(blocks):
        low, high = block * MOST, (block + 1) * MOST
        d_normed = dot_nt(dqkv[low:high, :], wb[...]) * gain_b
        widened = xb[low:high, :].astype(F32)
        scale = scales[block]
        pull = jnp.mean(d_normed * widened, axis=-1, keepdims=True) * scale * scale * scale
        termb[low:high, :] = (d_normed * scale - widened * pull).astype(BF16)
    start_edges(BWD, range(1, peers))
    send_own(BWD)
    for step in middle[1:]:
        pass_on(FWD, step)

    grad_copy = pltpu.make_async_remote_copy(
        src_ref=grad_out,
        dst_ref=grad_ref,
        send_sem=grad_sems.at[0],
        recv_sem=grad_sems.at[1],
        device_id=(pipes - 1 - p, t),
        device_id_type=MESH,
    )
    tile = 512
    for low in range(0, wide, tile):
        grad_out[:, low : low + tile] = dot_tn(att[...], c_ref[:, low : low + tile]).astype(BF16)
    grad_copy.start()

    pass_on(BWD, middle[0])
    finish(FWD, outf_ref)
    for step in middle[1:]:
        pass_on(BWD, step)
    grad_copy.wait_recv()
    finish(BWD, outb_ref)

    grad_copy.wait_send()

    @pl.when(sends)
    def left():
        for way in (FWD, BWD):
            own_copy(way).wait_send()
        for flow in (RIGHT, LEFT):
            for step in range(1, peers):

                @pl.when(places[flow] < step)
                def gone():
                    for way in (FWD, BWD):
                        for copy in chain_copies(flow, way, step, owner_at(flow, step)):
                            copy.wait_send()


ANY_SPEC = pl.BlockSpec(memory_space=pl.ANY)
VMEM_SPEC = pl.BlockSpec(memory_space=pltpu.VMEM)


def per_device(
    fwd_inputs,
    bwd_inputs,
    bwd_cotangent,
    fwd_lengths,
    bwd_lengths,
    norm_gains,
    query_weight,
    key_weight,
    value_weight,
    out_weight,
):
    pipes, peers = lax.axis_size("pipe"), lax.axis_size("tensor")
    rows, wide = fwd_inputs.shape[1:]
    width = query_weight.shape[3]
    share = rows // peers
    pieces = 3 if share % 48 == 0 and share > 48 else 1
    dma = pltpu.SemaphoreType.DMA
    moved, moved_grad, mirrored = pl.pallas_call(
        functools.partial(sections_kernel, pipes, peers, pieces),
        out_shape=(
            jax.ShapeDtypeStruct((share, wide), BF16),
            jax.ShapeDtypeStruct((share, wide), BF16),
            jax.ShapeDtypeStruct((width, wide), BF16),
        ),
        in_specs=[ANY_SPEC] * 10,
        out_specs=(VMEM_SPEC,) * 3,
        scratch_shapes=[
            pltpu.SMEM(fwd_lengths.shape, jnp.int32),
            pltpu.SMEM(bwd_lengths.shape, jnp.int32),
            pltpu.VMEM((2, wide), BF16),
            pltpu.VMEM((rows, wide), BF16),
            pltpu.VMEM((rows, wide), BF16),
            pltpu.VMEM((rows, wide), BF16),
            pltpu.VMEM((wide, 3 * width), BF16),
            pltpu.VMEM((wide, 3 * width), BF16),
            pltpu.VMEM((width, wide), BF16),
            pltpu.VMEM((width, wide), BF16),
            pltpu.VMEM((rows + MOST, 3 * width), BF16),
            pltpu.VMEM((rows, 3 * width), BF16),
            pltpu.VMEM((rows, 3 * width), BF16),
            pltpu.VMEM((rows, width), BF16),
            pltpu.VMEM((rows, wide), BF16),
            pltpu.VMEM((rows, wide), BF16),
            pltpu.VMEM((2, share, wide), BF16),
            pltpu.VMEM((width, wide), BF16),
            pltpu.VMEM((2, 2, peers - 2, share, wide), BF16),
            pltpu.VMEM((2, 2, share, wide), BF16),
            pltpu.VMEM((2, share, wide), BF16),
            dma((16,)),
            dma((2, 2, peers - 1, pieces)),
            dma((2, 2, peers - 1, pieces)),
            dma((2,)),
            dma((2,)),
            dma((2,)),
        ],
        compiler_params=pltpu.CompilerParams(
            collective_id=0, has_side_effects=True, vmem_limit_bytes=VMEM_LIMIT
        ),
        cost_estimate=pl.CostEstimate(
            flops=28 * rows * wide * width,
            bytes_accessed=16 * wide * (rows + width),
            transcendentals=2 * rows * MOST,
        ),
        name="sections",
    )(
        fwd_lengths,
        bwd_lengths,
        norm_gains.reshape(2, wide),
        fwd_inputs,
        bwd_inputs,
        bwd_cotangent,
        query_weight,
        key_weight,
        value_weight,
        out_weight,
    )
    return (moved[None], moved_grad[None], mirrored.astype(F32)[None])


def solution(mesh):
    placed = (
        P("pipe", None, None),
        P("pipe", None, None),
        P("pipe", None, None),
        P("pipe", None),
        P("pipe", None),
        P(None, "pipe", None),
        P(None, "pipe", None, "tensor"),
        P(None, "pipe", None, "tensor"),
        P(None, "pipe", None, "tensor"),
        P(None, "pipe", "tensor", None),
    )
    return jax.shard_map(
        per_device,
        mesh=mesh,
        in_specs=placed,
        out_specs=(P("pipe", "tensor", None), P("pipe", "tensor", None), P("pipe", "tensor", None)),
        check_vma=False,
    )
```

```python
import functools

import jax
import jax.numpy as jnp
from jax import lax
from jax.experimental import pallas as pl
from jax.experimental.pallas import tpu as pltpu
from jax.sharding import PartitionSpec as P

HEAD_DIM = 128
MOST = 192
VMEM_LIMIT = 54 * 1024 * 1024
MESH = pl.DeviceIdType.MESH
RIGHT, LEFT = 0, 1
FWD, BWD = 0, 1
F32 = jnp.float32
BF16 = jnp.bfloat16


def doc_start(lengths_ref, first_row, row_count):
    position = lax.broadcasted_iota(jnp.int32, (row_count, 1), 0) + first_row
    start = jnp.zeros((row_count, 1), jnp.int32)
    end = jnp.int32(0)
    for doc in range(lengths_ref.shape[1]):
        end = end + lengths_ref[0, doc]
        start = jnp.where(position >= end, end, start)
    return position, start


def window_mask(lengths_ref, first_row, row_count, first_key, key_count):
    position, start = doc_start(lengths_ref, first_row, row_count)
    keys = lax.broadcasted_iota(jnp.int32, (row_count, key_count), 1) + first_key
    return (keys >= start) & (keys <= position)


def dot_nn(left, right):
    return jnp.dot(left, right, preferred_element_type=F32)


def dot_nt(left, right):
    return lax.dot_general(left, right, (((1,), (1,)), ((), ())), preferred_element_type=F32)


def dot_tn(left, right):
    return lax.dot_general(left, right, (((0,), (0,)), ((), ())), preferred_element_type=F32)


def normed_rows(x, gain):
    widened = x.astype(F32)
    mean_square = jnp.mean(widened * widened, axis=-1, keepdims=True)
    scale = lax.rsqrt(mean_square + 1e-05)
    return (widened * scale * gain).astype(BF16), scale


def score_block(queries, key_rows, keep):
    scores = dot_nt(queries, key_rows) * HEAD_DIM ** (-0.5)
    scores = jnp.where(keep, scores, -1e30)
    weights = jnp.exp(scores - jnp.max(scores, axis=-1, keepdims=True))
    return weights, 1.0 / jnp.sum(weights, axis=-1, keepdims=True)


def rows_at(first, count):
    return pl.ds(pl.multiple_of(first, 16), count)


def lent_rows(pipes, peers, share):
    half = (pipes - 1) // 2
    return 16 if pipes > 2 and share > 64 and half * 16 <= share else 0


def sections_kernel(
    pipes, peers, pieces, lent,
    len_f_hbm, len_b_hbm, gain_hbm, xf_hbm, xb_hbm, c_hbm, wq_hbm, wk_hbm, wv_hbm, wo_hbm,
    outf_ref, outb_ref, grad_ref,
    lens_f, lens_b, gain_ref, xf, xb, c_ref, wf, wb, wof, wob, qkvf, qkvb, dqkv, att,
    term, own, grad_out, mid_recv, last_recv, help_recv,
    load_sem, chain_send, chain_recv, own_send_sem, own_recv_sem, grad_sems,
    help_sem, lent_send, lent_recv, back_send, back_recv,
):
    p = lax.axis_index("pipe")
    t = lax.axis_index("tensor")
    rows, wide = xf.shape
    width = wof.shape[0]
    heads = width // HEAD_DIM
    share = rows // peers
    blocks = rows // MOST
    last = peers - 1
    helper = pipes - 1
    lenders = pipes - 2 if lent else 0
    half = (lenders + 1) // 2
    kept = share - lent
    sends = p < helper
    takes = p > 0
    helps = p == helper
    lends = p < lenders

    if lent:
        classes = {
            FWD: [(lends, kept), (p == lenders, share)],
            BWD: [(sends, share)],
        }
    else:
        classes = {FWD: [(sends, share)], BWD: [(sends, share)]}
    helper_count = half * lent
    inputs = (xf, c_ref)
    finals = (1, pieces)

    slot = iter(range(load_sem.shape[0]))

    def load(source, target):
        return pltpu.make_async_copy(source, target, load_sem.at[next(slot)])

    low_half = t < peers // 2
    order = [jnp.where(low_half, blocks - 1 - i, i) for i in range(blocks)]
    pair_low = jnp.where(low_half, (blocks - 2) * MOST, 0)

    gain_copy = load(gain_hbm, gain_ref)
    lens_f_copy = load(len_f_hbm, lens_f)
    pair_at, third_at = rows_at(pair_low, 2 * MOST), rows_at(order[2] * MOST, MOST)
    x_copies = [load(xf_hbm.at[0, at], xf.at[at]) for at in (pair_at, third_at)]
    wf_copies = [
        load(source.at[0, 0], wf.at[:, part * width : (part + 1) * width])
        for part, source in enumerate((wq_hbm, wk_hbm, wv_hbm))
    ]
    wof_copy = load(wo_hbm.at[0, 0], wof)
    xb_copy = load(xb_hbm.at[0], xb)
    wb_copies = [
        load(source.at[1, 0], wb.at[:, part * width : (part + 1) * width])
        for part, source in enumerate((wq_hbm, wk_hbm, wv_hbm))
    ]
    c_copy = load(c_hbm.at[0], c_ref)
    wob_copy = load(wo_hbm.at[1, 0], wob)
    lens_b_copy = load(len_b_hbm, lens_b)

    gain_copy.start()

    @pl.when(sends)
    def load_forward():
        for copy in (lens_f_copy, x_copies[0], wf_copies[1], wf_copies[0], wf_copies[2]):
            copy.start()
        wof_copy.start()
        x_copies[1].start()

    barrier = pltpu.get_barrier_semaphore()
    to_right, to_left = t < last, t > 0
    chains = p >= 0 if lent else sends
    always = p >= 0
    roles = [
        (chains & to_right, chains & to_left, (p, t - 1)),
        (chains & to_left, chains & to_right, (p, t + 1)),
        (sends, takes, (p - 1, t)),
        (always, always, (helper - p, t)),
    ]
    for lender in range(lenders):
        roles.append((p == lender, helps, (lender, t)))
        roles.append((helps, p == lender + 1, (helper, t)))

    for unused, has_source, source in roles:

        @pl.when(has_source)
        def greet():
            pl.semaphore_signal(barrier, inc=1, device_id=source, device_id_type=MESH)

    def await_barrier():
        count = jnp.int32(0)
        for has_target, unused, unused_too in roles:
            count = count + has_target.astype(jnp.int32)
        pl.semaphore_wait(barrier, count)

    places = (t, last - t)

    def owner_at(flow, step):
        owner = peers - step + places[flow]
        return owner if flow == RIGHT else last - owner

    def parts_of(way, step, aid):
        return pieces if way == BWD and not aid else 1

    def chain_copy(flow, way, step, owner, count, part=0, aid=False):
        toward = t + 1 if flow == RIGHT else t - 1
        size = count // parts_of(way, step, aid)
        device = (p, toward)
        recv_sem = chain_recv.at[flow, way, step - 1, part]
        if step < last:
            target = mid_recv.at[flow, way, step - 1, part * size : (part + 1) * size]
        elif aid:
            target = help_recv.at[flow, way]
            recv_sem = help_sem.at[flow, way]
        else:
            target = last_recv.at[flow, way, part * size : (part + 1) * size]
        return pltpu.make_async_remote_copy(
            src_ref=term.at[way, rows_at(owner * share + part * size, size)],
            dst_ref=target,
            send_sem=chain_send.at[flow, way, step - 1, part],
            recv_sem=recv_sem,
            device_id=device,
            device_id_type=MESH,
        )

    def edge_copies(flow, way, step, count, aid=False):
        owner = peers - step if flow == RIGHT else step - 1
        return [
            chain_copy(flow, way, step, owner, count, part, aid)
            for part in range(parts_of(way, step, aid))
        ]

    def start_edges(way, steps):
        for flow in (RIGHT, LEFT):
            for member, count in classes[way]:

                @pl.when(member & (places[flow] == 0))
                def start():
                    for step in steps:
                        for copy in edge_copies(flow, way, step, count):
                            copy.start()

    def pass_block(flow, way, step, count, aid=False):
        owner = owner_at(flow, step)
        parts = parts_of(way, step, aid)
        size = count // parts
        for part in range(parts):
            chain_copy(flow, way, step - 1, owner, count, part, aid).wait_recv()
            at = rows_at(owner * share + part * size, size)
            arrived = mid_recv[flow, way, step - 2, part * size : (part + 1) * size, :]
            total = term[way, at, :].astype(F32) + arrived.astype(F32)
            term[way, at, :] = total.astype(BF16)
            chain_copy(flow, way, step, owner, count, part, aid).start()

    def pass_on(way, step):
        turns = ((LEFT, low_half), (RIGHT, None), (LEFT, jnp.logical_not(low_half)))
        for flow, turn in turns:
            here = places[flow]
            for member, count in classes[way]:
                condition = member & (here >= 1) & (here < step)
                condition = condition if turn is None else condition & turn

                @pl.when(condition)
                def add():
                    pass_block(flow, way, step, count)

    def own_copy(way, count, part=0):
        size = count // finals[way]
        at = slice(part * size, (part + 1) * size)
        return pltpu.make_async_remote_copy(
            src_ref=own.at[way, at],
            dst_ref=(outf_ref, outb_ref)[way].at[at],
            send_sem=own_send_sem.at[way, part],
            recv_sem=own_recv_sem.at[way, part],
            device_id=(p + 1, t),
            device_id_type=MESH,
        )

    def finish(way):
        for member, count in classes[way]:

            @pl.when(member)
            def sum_up():
                size = count // finals[way]
                for part in range(finals[way]):
                    for flow in (RIGHT, LEFT):

                        @pl.when(places[flow] >= 1)
                        def arrive():
                            chain_copy(flow, way, last, t, count, part).wait_recv()

                    at = slice(part * size, (part + 1) * size)
                    here = rows_at(t * share + part * size, size)
                    total = inputs[way][here, :].astype(F32) + term[way, here, :].astype(F32)
                    for flow in (RIGHT, LEFT):
                        total = total + last_recv[flow, way, at].astype(F32)
                    own[way, at, :] = total.astype(BF16)
                    own_copy(way, count, part).start()

    def lent_copy(lender, owner):
        to_way, place = lender // max(half, 1), lax.rem(lender, max(half, 1))
        return pltpu.make_async_remote_copy(
            src_ref=term.at[FWD, rows_at(owner * share + kept, lent)],
            dst_ref=term.at[to_way, rows_at(owner * share + place * lent, lent)],
            send_sem=lent_send.at[owner],
            recv_sem=lent_recv.at[lender, owner],
            device_id=(helper, t),
            device_id_type=MESH,
        )

    def lend():
        @pl.when(lends)
        def hand_over():
            at = rows_at(t * share + kept, lent)
            total = xf[at, :].astype(F32) + term[FWD, at, :].astype(F32)
            term[FWD, at, :] = total.astype(BF16)
            for owner in range(peers):
                lent_copy(p, owner).start()

    def back_copy(lender):
        way, place = lender // half, lender % half
        return pltpu.make_async_remote_copy(
            src_ref=own.at[way, place * lent : (place + 1) * lent],
            dst_ref=outf_ref.at[kept:share],
            send_sem=back_send.at[lender],
            recv_sem=back_recv,
            device_id=(lender + 1, t),
            device_id_type=MESH,
        )

    def carry_for_lenders():
        count = helper_count
        ways = (FWD, BWD)
        for way in ways:
            for lender in range(way * half, min((way + 1) * half, lenders)):
                for owner in range(peers):
                    lent_copy(lender, owner).wait_recv()
            for flow in (RIGHT, LEFT):

                @pl.when(places[flow] == 0)
                def start():
                    for copy in edge_copies(flow, way, 1, count, True):
                        copy.start()

        for step in range(2, peers):
            for way in ways:
                for flow in (RIGHT, LEFT):

                    @pl.when(places[flow] == 0)
                    def start():
                        for copy in edge_copies(flow, way, step, count, True):
                            copy.start()

                    @pl.when((places[flow] >= 1) & (places[flow] < step))
                    def add():
                        pass_block(flow, way, step, count, True)

        for way in ways:
            for flow in (RIGHT, LEFT):

                @pl.when(places[flow] >= 1)
                def arrive():
                    chain_copy(flow, way, last, t, count, 0, True).wait_recv()

            total = term[way, rows_at(t * share, count), :].astype(F32)
            for flow in (RIGHT, LEFT):
                total = total + help_recv[flow, way].astype(F32)
            own[way, 0:count, :] = total.astype(BF16)
            for lender in range(way * half, min((way + 1) * half, lenders)):
                back_copy(lender).start()

    qkvf[0:MOST, :] = jnp.zeros((MOST, 3 * width), BF16)
    gain_copy.wait()
    gain_f = gain_ref[0:1, :].astype(F32)
    gain_b = gain_ref[1:2, :].astype(F32)

    def attend_forward(i):
        low = order[i] * MOST
        query_at = rows_at(low + MOST, MOST)
        key_at = rows_at(low, 2 * MOST)
        keep = window_mask(lens_f, low, MOST, low - MOST, 2 * MOST)
        parts = []
        for head in range(heads):
            at = head * HEAD_DIM
            weights, inverse = score_block(
                qkvf[query_at, at : at + HEAD_DIM],
                qkvf[key_at, width + at : width + at + HEAD_DIM],
                keep,
            )
            mixed = dot_nn(
                (weights * inverse).astype(BF16),
                qkvf[key_at, 2 * width + at : 2 * width + at + HEAD_DIM],
            )
            parts.append(mixed.astype(BF16))
        attended = jnp.concatenate(parts, axis=1)
        if i == 0:
            wof_copy.wait()
        term[FWD, rows_at(low, MOST), :] = dot_nn(attended, wof[...]).astype(BF16)

    def load_backward():
        for copy in (xb_copy, *wb_copies, lens_b_copy, c_copy, wob_copy):
            copy.start()

    @pl.when(sends)
    def forward_first():
        x_copies[0].wait()
        normed, unused = normed_rows(xf[pair_at, :], gain_f)
        for part in (1, 0, 2):
            cols = slice(part * width, (part + 1) * width)
            wf_copies[part].wait()
            qkvf[rows_at(pair_low + MOST, 2 * MOST), cols] = dot_nn(normed, wf[:, cols]).astype(BF16)
        lens_f_copy.wait()
        attend_forward(0)

    await_barrier()
    start_edges(FWD, [1])
    load_backward()

    @pl.when(sends)
    def forward_rest():
        x_copies[1].wait()
        normed, unused = normed_rows(xf[third_at, :], gain_f)
        qkvf[rows_at((order[2] + 1) * MOST, MOST), :] = dot_nn(normed, wf[...]).astype(BF16)
        attend_forward(1)
        attend_forward(2)

    if lent:
        lend()
    start_edges(FWD, range(2, peers))

    zeros = jnp.zeros((share, wide), BF16)

    @pl.when(jnp.logical_not(takes))
    def clear_results():
        outf_ref[...] = zeros
        outb_ref[...] = zeros

    for flow in (RIGHT, LEFT):

        @pl.when(places[flow] == 0)
        def clear_last():
            for way in (FWD, BWD):
                last_recv[flow, way] = zeros
                if lent:
                    help_recv[flow, way] = jnp.zeros((helper_count, wide), BF16)

    xb_copy.wait()
    scales = []
    for block in range(blocks):
        low, high = block * MOST, (block + 1) * MOST
        normed, scale = normed_rows(xb[low:high, :], gain_b)
        scales.append(scale)
        if block == 0:
            for copy in wb_copies:
                copy.wait()
        qkvb[low:high, :] = dot_nn(normed, wb[...]).astype(BF16)
    c_copy.wait()
    wob_copy.wait()
    lens_b_copy.wait()
    middle = [step for step in range(2, peers)]
    carried = {}
    for block in range(blocks):
        low, high = block * MOST, (block + 1) * MOST
        key_low = max(0, low - MOST)
        keep = window_mask(lens_b, low, MOST, key_low, high - key_low)
        d_attended = dot_nt(c_ref[low:high, :], wob[...]).astype(BF16)
        for head in range(heads):
            at = head * HEAD_DIM
            cols = [slice(part * width + at, part * width + at + HEAD_DIM) for part in range(3)]
            queries = qkvb[low:high, cols[0]]
            key_rows = qkvb[key_low:high, cols[1]]
            value_rows = qkvb[key_low:high, cols[2]]
            weights, inverse = score_block(queries, key_rows, keep)
            probs = weights * inverse
            probs_bf = probs.astype(BF16)
            mixed = dot_nn(probs_bf, value_rows)
            att[low:high, at : at + HEAD_DIM] = mixed.astype(BF16)
            d_mixed = d_attended[:, at : at + HEAD_DIM]
            d_probs = dot_nt(d_mixed, value_rows)
            delta = jnp.sum(mixed * d_mixed.astype(F32), axis=-1, keepdims=True)
            d_scores = (probs * (d_probs - delta) * HEAD_DIM ** (-0.5)).astype(BF16)
            dqkv[low:high, cols[0]] = dot_nn(d_scores, key_rows).astype(BF16)
            d_keys = dot_tn(d_scores, queries)
            d_values = dot_tn(probs_bf, d_mixed)
            if block > 0:
                past_keys, past_values = carried[head]
                dqkv[key_low:low, cols[1]] = (past_keys + d_keys[:MOST]).astype(BF16)
                dqkv[key_low:low, cols[2]] = (past_values + d_values[:MOST]).astype(BF16)
                d_keys, d_values = d_keys[MOST:], d_values[MOST:]
            if block == blocks - 1:
                dqkv[low:high, cols[1]] = d_keys.astype(BF16)
                dqkv[low:high, cols[2]] = d_values.astype(BF16)
            carried[head] = (d_keys, d_values)
        if block == 0:
            pass_on(FWD, middle[0])
    grad_copy = pltpu.make_async_remote_copy(
        src_ref=grad_out,
        dst_ref=grad_ref,
        send_sem=grad_sems.at[0],
        recv_sem=grad_sems.at[1],
        device_id=(pipes - 1 - p, t),
        device_id_type=MESH,
    )
    early = always

    def start_grad(condition):
        @pl.when(condition)
        def start():
            grad_copy.start()

    tile = 512
    for low in range(0, wide, tile):
        grad_out[:, low : low + tile] = dot_tn(att[...], c_ref[:, low : low + tile]).astype(BF16)
    start_grad(early)

    @pl.when(sends)
    def input_terms():
        for block in range(blocks):
            low, high = block * MOST, (block + 1) * MOST
            d_normed = dot_nt(dqkv[low:high, :], wb[...]) * gain_b
            widened = xb[low:high, :].astype(F32)
            scale = scales[block]
            pull = jnp.mean(d_normed * widened, axis=-1, keepdims=True) * scale * scale * scale
            term[BWD, low:high, :] = (d_normed * scale - widened * pull).astype(BF16)
        start_edges(BWD, range(1, peers))
        start_grad(jnp.logical_not(early))

    for step in middle[1:]:
        pass_on(FWD, step)
    if lent:
        pl.when(helps)(carry_for_lenders)
    pass_on(BWD, middle[0])
    finish(FWD)
    for step in middle[1:]:
        pass_on(BWD, step)

    finish(BWD)
    grad_copy.wait_recv()

    @pl.when(takes)
    def forward_landed():
        if lent:

            @pl.when(helps)
            def whole():
                own_copy(FWD, share).wait_recv()

            @pl.when(sends)
            def both():
                own_copy(FWD, kept).wait_recv()
                back_copy(0).wait_recv()

        else:
            own_copy(FWD, share).wait_recv()

    @pl.when(takes)
    def backward_landed():
        for part in range(finals[BWD]):
            own_copy(BWD, share, part).wait_recv()

    grad_copy.wait_send()
    for way in (FWD, BWD):
        for member, count in classes[way]:

            @pl.when(member)
            def own_left():
                for part in range(finals[way]):
                    own_copy(way, count, part).wait_send()

    if lent:

        @pl.when(lends)
        def lent_left():
            for owner in range(peers):
                lent_copy(p, owner).wait_send()

        @pl.when(helps)
        def back_left():
            for lender in range(lenders):
                back_copy(lender).wait_send()

    for flow in (RIGHT, LEFT):
        for way in (FWD, BWD):
            groups = [(member, count, False) for member, count in classes[way]]
            if lent:
                groups.append((helps, helper_count, True))
            for member, count, aid in groups:
                for step in range(1, peers):

                    @pl.when(member & (places[flow] < step))
                    def gone():
                        for part in range(parts_of(way, step, aid)):
                            chain_copy(
                                flow, way, step, owner_at(flow, step), count, part, aid
                            ).wait_send()


HBM_SPEC = pl.BlockSpec(memory_space=pltpu.HBM)
VMEM_SPEC = pl.BlockSpec(memory_space=pltpu.VMEM)


def results_kernel(
    moved_ref, moved_grad_ref, mirrored_ref, out_hbm, out_grad_hbm, weight_hbm, wide_ref, sems
):
    copies = [
        pltpu.make_async_copy(moved_ref, out_hbm.at[0], sems.at[0]),
        pltpu.make_async_copy(moved_grad_ref, out_grad_hbm.at[0], sems.at[1]),
    ]
    for copy in copies:
        copy.start()
    parts = sems.shape[0] - 2
    size = wide_ref.shape[0] // parts
    for part in range(parts):
        at = slice(part * size, (part + 1) * size)
        wide_ref[at, :] = mirrored_ref[at, :].astype(F32)
        copy = pltpu.make_async_copy(wide_ref.at[at], weight_hbm.at[0, at], sems.at[2 + part])
        copy.start()
        copies.append(copy)
    for copy in copies:
        copy.wait()


def results_of(moved, moved_grad, mirrored):
    share, wide = moved.shape
    width = mirrored.shape[0]
    parts = 4
    return pl.pallas_call(
        results_kernel,
        out_shape=(
            jax.ShapeDtypeStruct((1, share, wide), BF16),
            jax.ShapeDtypeStruct((1, share, wide), BF16),
            jax.ShapeDtypeStruct((1, width, wide), F32),
        ),
        in_specs=[VMEM_SPEC] * 3,
        out_specs=(HBM_SPEC,) * 3,
        scratch_shapes=[pltpu.VMEM((width, wide), F32), pltpu.SemaphoreType.DMA((2 + parts,))],
        compiler_params=pltpu.CompilerParams(vmem_limit_bytes=8 * 1024 * 1024),
        name="results",
    )(moved, moved_grad, mirrored)


def per_device(
    fwd_inputs,
    bwd_inputs,
    bwd_cotangent,
    fwd_lengths,
    bwd_lengths,
    norm_gains,
    query_weight,
    key_weight,
    value_weight,
    out_weight,
):
    pipes, peers = lax.axis_size("pipe"), lax.axis_size("tensor")
    rows, wide = fwd_inputs.shape[1:]
    width = query_weight.shape[3]
    share = rows // peers
    pieces = 3 if share % 48 == 0 and share > 48 else 1
    lent = lent_rows(pipes, peers, share)
    lenders = pipes - 2 if lent else 1
    helper_count = max((lenders + 1) // 2 * lent, 16)
    dma = pltpu.SemaphoreType.DMA
    moved, moved_grad, mirrored = pl.pallas_call(
        functools.partial(sections_kernel, pipes, peers, pieces, lent),
        out_shape=(
            pltpu.VMEM((share, wide), BF16),
            pltpu.VMEM((share, wide), BF16),
            pltpu.VMEM((width, wide), BF16),
        ),
        in_specs=[HBM_SPEC] * 10,
        out_specs=(VMEM_SPEC,) * 3,
        scratch_shapes=[
            pltpu.SMEM(fwd_lengths.shape, jnp.int32),
            pltpu.SMEM(bwd_lengths.shape, jnp.int32),
            pltpu.VMEM((2, wide), BF16),
            pltpu.VMEM((rows, wide), BF16),
            pltpu.VMEM((rows, wide), BF16),
            pltpu.VMEM((rows, wide), BF16),
            pltpu.VMEM((wide, 3 * width), BF16),
            pltpu.VMEM((wide, 3 * width), BF16),
            pltpu.VMEM((width, wide), BF16),
            pltpu.VMEM((width, wide), BF16),
            pltpu.VMEM((rows + MOST, 3 * width), BF16),
            pltpu.VMEM((rows, 3 * width), BF16),
            pltpu.VMEM((rows, 3 * width), BF16),
            pltpu.VMEM((rows, width), BF16),
            pltpu.VMEM((2, rows, wide), BF16),
            pltpu.VMEM((2, share, wide), BF16),
            pltpu.VMEM((width, wide), BF16),
            pltpu.VMEM((2, 2, peers - 2, share, wide), BF16),
            pltpu.VMEM((2, 2, share, wide), BF16),
            pltpu.VMEM((2, 2, helper_count, wide), BF16),
            dma((16,)),
            dma((2, 2, peers - 1, pieces)),
            dma((2, 2, peers - 1, pieces)),
            dma((2, pieces)),
            dma((2, pieces)),
            dma((2,)),
            dma((2, 2)),
            dma((peers,)),
            dma((lenders, peers)),
            dma((lenders,)),
            dma,
        ],
        compiler_params=pltpu.CompilerParams(
            collective_id=0, has_side_effects=True, vmem_limit_bytes=VMEM_LIMIT
        ),
        cost_estimate=pl.CostEstimate(
            flops=28 * rows * wide * width,
            bytes_accessed=16 * wide * (rows + width),
            transcendentals=2 * rows * MOST,
        ),
        name="sections",
    )(
        fwd_lengths,
        bwd_lengths,
        norm_gains.reshape(2, wide),
        fwd_inputs,
        bwd_inputs,
        bwd_cotangent,
        query_weight,
        key_weight,
        value_weight,
        out_weight,
    )
    return results_of(moved, moved_grad, mirrored)


def solution(mesh):
    placed = (
        P("pipe", None, None),
        P("pipe", None, None),
        P("pipe", None, None),
        P("pipe", None),
        P("pipe", None),
        P(None, "pipe", None),
        P(None, "pipe", None, "tensor"),
        P(None, "pipe", None, "tensor"),
        P(None, "pipe", None, "tensor"),
        P(None, "pipe", "tensor", None),
    )
    return jax.shard_map(
        per_device,
        mesh=mesh,
        in_specs=placed,
        out_specs=(P("pipe", "tensor", None), P("pipe", "tensor", None), P("pipe", "tensor", None)),
        check_vma=False,
    )
```

```python
import functools

import jax
import jax.numpy as jnp
from jax import lax
from jax.experimental import pallas as pl
from jax.experimental.pallas import tpu as pltpu
from jax.sharding import PartitionSpec as P

HEAD_DIM = 128
MOST = 192
VMEM_LIMIT = 54 * 1024 * 1024
MESH = pl.DeviceIdType.MESH
RIGHT, LEFT = 0, 1
FWD, BWD = 0, 1
F32 = jnp.float32
BF16 = jnp.bfloat16


def doc_start(lengths_ref, first_row, row_count):
    position = lax.broadcasted_iota(jnp.int32, (row_count, 1), 0) + first_row
    start = jnp.zeros((row_count, 1), jnp.int32)
    end = jnp.int32(0)
    for doc in range(lengths_ref.shape[1]):
        end = end + lengths_ref[0, doc]
        start = jnp.where(position >= end, end, start)
    return position, start


def window_mask(lengths_ref, first_row, row_count, first_key, key_count):
    position, start = doc_start(lengths_ref, first_row, row_count)
    keys = lax.broadcasted_iota(jnp.int32, (row_count, key_count), 1) + first_key
    return (keys >= start) & (keys <= position)


def dot_nn(left, right):
    return jnp.dot(left, right, preferred_element_type=F32)


def dot_nt(left, right):
    return lax.dot_general(left, right, (((1,), (1,)), ((), ())), preferred_element_type=F32)


def dot_tn(left, right):
    return lax.dot_general(left, right, (((0,), (0,)), ((), ())), preferred_element_type=F32)


def normed_rows(x, gain):
    widened = x.astype(F32)
    mean_square = jnp.mean(widened * widened, axis=-1, keepdims=True)
    scale = lax.rsqrt(mean_square + 1e-05)
    return (widened * scale * gain).astype(BF16), scale


def score_block(queries, key_rows, keep):
    scores = dot_nt(queries, key_rows) * HEAD_DIM ** (-0.5)
    scores = jnp.where(keep, scores, -1e30)
    weights = jnp.exp(scores - jnp.max(scores, axis=-1, keepdims=True))
    return weights, 1.0 / jnp.sum(weights, axis=-1, keepdims=True)


def rows_at(first, count):
    return pl.ds(pl.multiple_of(first, 16), count)


def lent_rows(pipes, peers, share):
    half = (pipes - 1) // 2
    return 32 if pipes > 2 and share > 64 and half * 32 <= share else 0


def sections_kernel(
    pipes, peers, lent,
    len_f_hbm, len_b_hbm, gain_hbm, xf_hbm, xb_hbm, c_hbm, wq_hbm, wk_hbm, wv_hbm, wo_hbm,
    outf_ref, outb_ref, grad_ref,
    lens_f, lens_b, gain_ref, xf, xb, c_ref, wf, wb, wof, wob, qkvf, qkvb, dqkv, att,
    term, own, grad_out, mid_recv, last_recv, help_recv,
    load_sem, chain_send, chain_recv, own_send_sem, own_recv_sem, grad_sems,
    help_sem, lent_send, lent_recv, back_send, back_recv,
):
    p = lax.axis_index("pipe")
    t = lax.axis_index("tensor")
    rows, wide = xf.shape
    width = wof.shape[0]
    heads = width // HEAD_DIM
    share = rows // peers
    blocks = rows // MOST
    last = peers - 1
    helper = pipes - 1
    lenders = pipes - 2 if lent else 0
    half = (lenders + 1) // 2
    kept = share - lent
    sends = p < helper
    takes = p > 0
    helps = p == helper
    lends = p < lenders

    if lent:
        classes = {
            FWD: [(lends, kept), (p == lenders, share)],
            BWD: [(sends, share)],
        }
    else:
        classes = {FWD: [(sends, share)], BWD: [(sends, share)]}
    helper_count = half * lent
    inputs = (xf, c_ref)

    slot = iter(range(load_sem.shape[0]))

    def load(source, target):
        return pltpu.make_async_copy(source, target, load_sem.at[next(slot)])

    low_half = t < peers // 2
    order = [jnp.where(low_half, blocks - 1 - i, i) for i in range(blocks)]
    pair_low = jnp.where(low_half, (blocks - 2) * MOST, 0)

    gain_copy = load(gain_hbm, gain_ref)
    lens_f_copy = load(len_f_hbm, lens_f)
    pair_at, third_at = rows_at(pair_low, 2 * MOST), rows_at(order[2] * MOST, MOST)
    x_copies = [load(xf_hbm.at[0, at], xf.at[at]) for at in (pair_at, third_at)]
    wf_copies = [
        load(source.at[0, 0], wf.at[:, part * width : (part + 1) * width])
        for part, source in enumerate((wq_hbm, wk_hbm, wv_hbm))
    ]
    wof_copy = load(wo_hbm.at[0, 0], wof)
    xb_copy = load(xb_hbm.at[0], xb)
    wb_copies = [
        load(source.at[1, 0], wb.at[:, part * width : (part + 1) * width])
        for part, source in enumerate((wq_hbm, wk_hbm, wv_hbm))
    ]
    c_copy = load(c_hbm.at[0], c_ref)
    wob_copy = load(wo_hbm.at[1, 0], wob)
    lens_b_copy = load(len_b_hbm, lens_b)

    gain_copy.start()

    @pl.when(sends)
    def load_forward():
        for copy in (x_copies[0], wf_copies[1], wf_copies[0], wf_copies[2], lens_f_copy, wof_copy):
            copy.start()
        x_copies[1].start()

    barrier = pltpu.get_barrier_semaphore()
    to_right, to_left = t < last, t > 0
    chains = p >= 0 if lent else sends
    always = p >= 0
    roles = [
        (chains & to_right, chains & to_left, (p, t - 1)),
        (chains & to_left, chains & to_right, (p, t + 1)),
        (sends, takes, (p - 1, t)),
        (always, always, (helper - p, t)),
    ]
    for lender in range(lenders):
        roles.append((p == lender, helps, (lender, t)))
        roles.append((helps, p == lender + 1, (helper, t)))

    for unused, has_source, source in roles:

        @pl.when(has_source)
        def greet():
            pl.semaphore_signal(barrier, inc=1, device_id=source, device_id_type=MESH)

    def await_barrier():
        count = jnp.int32(0)
        for has_target, unused, unused_too in roles:
            count = count + has_target.astype(jnp.int32)
        pl.semaphore_wait(barrier, count)

    places = (t, last - t)

    def owner_at(flow, step):
        owner = peers - step + places[flow]
        return owner if flow == RIGHT else last - owner

    def spans(way, count, aid=False):
        if aid:
            return [(at, lent) for at in range(0, count, lent)]
        if share <= 64:
            return [(0, count)]
        if way == FWD:
            return [(0, 64), (64, count - 64)]
        tail = (48, 16)
        return [(0, count - sum(tail)), (count - sum(tail), tail[0]), (count - tail[1], tail[1])]

    def chain_copy(flow, way, step, owner, span, part=0, aid=False):
        toward = t + 1 if flow == RIGHT else t - 1
        first, size = span
        recv_sem = chain_recv.at[flow, way, step - 1, part]
        if step < last:
            target = mid_recv.at[flow, way, step - 1, first : first + size]
        elif aid:
            target = help_recv.at[flow, way, first : first + size]
            recv_sem = help_sem.at[flow, way, part]
        else:
            target = last_recv.at[flow, way, first : first + size]
        return pltpu.make_async_remote_copy(
            src_ref=term.at[way, rows_at(owner * share + first, size)],
            dst_ref=target,
            send_sem=chain_send.at[flow, way, step - 1, part],
            recv_sem=recv_sem,
            device_id=(p, toward),
            device_id_type=MESH,
        )

    def start_edges(way, steps, only=None):
        for flow in (RIGHT, LEFT):
            for member, count in classes[way]:
                parts = range(len(spans(way, count))) if only is None else only
                parts = [part for part in parts if part < len(spans(way, count))]

                @pl.when(member & (places[flow] == 0))
                def start():
                    for step in steps:
                        owner = peers - step if flow == RIGHT else step - 1
                        for part in parts:
                            span = spans(way, count)[part]
                            chain_copy(flow, way, step, owner, span, part).start()

    def pass_part(flow, way, step, span, part, aid=False):
        owner = owner_at(flow, step)
        first, size = span
        chain_copy(flow, way, step - 1, owner, span, part, aid).wait_recv()
        at = rows_at(owner * share + first, size)
        arrived = mid_recv[flow, way, step - 2, first : first + size, :]
        total = term[way, at, :].astype(F32) + arrived.astype(F32)
        term[way, at, :] = total.astype(BF16)
        chain_copy(flow, way, step, owner, span, part, aid).start()

    turns = ((LEFT, low_half), (RIGHT, always), (LEFT, jnp.logical_not(low_half)))

    def pass_on(way, step):
        for flow, turn in turns:
            here = places[flow]
            for member, count in classes[way]:

                @pl.when(member & turn & (here >= 1) & (here < step))
                def add():
                    for part, span in enumerate(spans(way, count)):
                        pass_part(flow, way, step, span, part)

    def own_copy(way, span, part):
        at = slice(span[0], span[0] + span[1])
        return pltpu.make_async_remote_copy(
            src_ref=own.at[way, at],
            dst_ref=(outf_ref, outb_ref)[way].at[at],
            send_sem=own_send_sem.at[way, part],
            recv_sem=own_recv_sem.at[way, part],
            device_id=(p + 1, t),
            device_id_type=MESH,
        )

    def finish(way):
        for member, count in classes[way]:

            @pl.when(member)
            def sum_up():
                for part, span in enumerate(spans(way, count)):
                    first, size = span
                    for flow in (RIGHT, LEFT):

                        @pl.when(places[flow] >= 1)
                        def arrive():
                            chain_copy(flow, way, last, t, span, part).wait_recv()

                    at = slice(first, first + size)
                    here = rows_at(t * share + first, size)
                    total = inputs[way][here, :].astype(F32) + term[way, here, :].astype(F32)
                    for flow in (RIGHT, LEFT):
                        total = total + last_recv[flow, way, at].astype(F32)
                    own[way, at, :] = total.astype(BF16)
                    own_copy(way, span, part).start()

    def lent_copy(lender, owner):
        to_way, place = lender // max(half, 1), lax.rem(lender, max(half, 1))
        return pltpu.make_async_remote_copy(
            src_ref=term.at[FWD, rows_at(owner * share + kept, lent)],
            dst_ref=term.at[to_way, rows_at(owner * share + place * lent, lent)],
            send_sem=lent_send.at[owner],
            recv_sem=lent_recv.at[lender, owner],
            device_id=(helper, t),
            device_id_type=MESH,
        )

    def lend(owner):
        @pl.when(lends & (owner == t))
        def own_input():
            at = rows_at(t * share + kept, lent)
            total = xf[at, :].astype(F32) + term[FWD, at, :].astype(F32)
            term[FWD, at, :] = total.astype(BF16)

        @pl.when(lends)
        def hand_over():
            lent_copy(p, owner).start()

    def back_copy(lender):
        way, place = lender // half, lender % half
        return pltpu.make_async_remote_copy(
            src_ref=own.at[way, place * lent : (place + 1) * lent],
            dst_ref=outf_ref.at[kept:share],
            send_sem=back_send.at[lender],
            recv_sem=back_recv,
            device_id=(lender + 1, t),
            device_id_type=MESH,
        )

    def carry_for_lenders():
        jobs = [
            (lender, lender // half, lender % half, (lender % half * lent, lent))
            for lender in range(lenders)
        ]

        def start_edge(way, step, span, part):
            for flow in (RIGHT, LEFT):

                @pl.when(places[flow] == 0)
                def start():
                    owner = peers - step if flow == RIGHT else step - 1
                    chain_copy(flow, way, step, owner, span, part, True).start()

        for lender, way, part, span in jobs:
            for owner in range(peers):
                lent_copy(lender, owner).wait_recv()
            start_edge(way, 1, span, part)
        for step in range(2, peers):
            for unused, way, part, span in jobs:
                start_edge(way, step, span, part)
            for flow, turn in turns:

                @pl.when(turn & (places[flow] >= 1) & (places[flow] < step))
                def add():
                    for unused, way, part, span in jobs:
                        pass_part(flow, way, step, span, part, True)

        for lender, way, part, span in jobs:
            for flow in (RIGHT, LEFT):

                @pl.when(places[flow] >= 1)
                def arrive():
                    chain_copy(flow, way, last, t, span, part, True).wait_recv()

            at = slice(span[0], span[0] + lent)
            total = term[way, rows_at(t * share + span[0], lent), :].astype(F32)
            for flow in (RIGHT, LEFT):
                total = total + help_recv[flow, way, at].astype(F32)
            own[way, at, :] = total.astype(BF16)
            back_copy(lender).start()

    qkvf[0:MOST, :] = jnp.zeros((MOST, 3 * width), BF16)
    gain_copy.wait()
    gain_f = gain_ref[0:1, :].astype(F32)
    gain_b = gain_ref[1:2, :].astype(F32)

    def attend_forward(low, count):
        window = -(-(count + MOST - 1) // 128) * 128
        first_key = jnp.maximum(low + count - window, -MOST)
        query_at = rows_at(low + MOST, count)
        key_at = rows_at(first_key + MOST, window)
        keep = window_mask(lens_f, low, count, first_key, window)
        parts = []
        for head in range(heads):
            at = head * HEAD_DIM
            weights, inverse = score_block(
                qkvf[query_at, at : at + HEAD_DIM],
                qkvf[key_at, width + at : width + at + HEAD_DIM],
                keep,
            )
            mixed = dot_nn(
                (weights * inverse).astype(BF16),
                qkvf[key_at, 2 * width + at : 2 * width + at + HEAD_DIM],
            )
            parts.append(mixed.astype(BF16))
        attended = jnp.concatenate(parts, axis=1)
        term[FWD, rows_at(low, count), :] = dot_nn(attended, wof[...]).astype(BF16)

    def load_backward():
        for copy in (xb_copy, *wb_copies, lens_b_copy, c_copy, wob_copy):
            copy.start()

    @pl.when(sends)
    def forward_first():
        x_copies[0].wait()
        normed, unused = normed_rows(xf[pair_at, :], gain_f)
        for part in (1, 0, 2):
            cols = slice(part * width, (part + 1) * width)
            wf_copies[part].wait()
            qkvf[rows_at(pair_low + MOST, 2 * MOST), cols] = dot_nn(normed, wf[:, cols]).astype(BF16)
        lens_f_copy.wait()
        wof_copy.wait()

    def first_attention(low, count):
        @pl.when(sends)
        def attend():
            attend_forward(low, count)

    by_owner = share > 64
    if by_owner:
        turn = [jnp.where(low_half, last - i, i) for i in range(peers)]
        first_attention(turn[0] * share, 64)
    else:
        first_attention(order[0] * MOST, MOST)
    await_barrier()
    start_edges(FWD, [1], [0])
    if by_owner:
        first_attention(turn[0] * share + 64, share - 64)
        start_edges(FWD, [1], [1])
        if lent:
            lend(turn[0])
    load_backward()

    @pl.when(sends)
    def project_rest():
        x_copies[1].wait()
        normed, unused = normed_rows(xf[third_at, :], gain_f)
        qkvf[rows_at((order[2] + 1) * MOST, MOST), :] = dot_nn(normed, wf[...]).astype(BF16)

    if by_owner:
        for i in range(1, peers):
            first_attention(turn[i] * share, share)
            if i < last:
                start_edges(FWD, [i + 1])
            if lent:
                lend(turn[i])
    else:
        for i in range(1, blocks):
            first_attention(order[i] * MOST, MOST)
        start_edges(FWD, range(2, peers))

    zeros = jnp.zeros((share, wide), BF16)

    @pl.when(jnp.logical_not(takes))
    def clear_results():
        outf_ref[...] = zeros
        outb_ref[...] = zeros

    for flow in (RIGHT, LEFT):

        @pl.when(places[flow] == 0)
        def clear_last():
            for way in (FWD, BWD):
                last_recv[flow, way] = zeros
                if lent:
                    help_recv[flow, way] = jnp.zeros((helper_count, wide), BF16)

    xb_copy.wait()
    scales = []
    for block in range(blocks):
        low, high = block * MOST, (block + 1) * MOST
        normed, scale = normed_rows(xb[low:high, :], gain_b)
        scales.append(scale)
        if block == 0:
            for copy in wb_copies:
                copy.wait()
        qkvb[low:high, :] = dot_nn(normed, wb[...]).astype(BF16)
    c_copy.wait()
    wob_copy.wait()
    lens_b_copy.wait()
    middle = [step for step in range(2, peers)]
    carried = {}
    for block in range(blocks):
        low, high = block * MOST, (block + 1) * MOST
        key_low = max(0, low - MOST)
        keep = window_mask(lens_b, low, MOST, key_low, high - key_low)
        d_attended = dot_nt(c_ref[low:high, :], wob[...]).astype(BF16)
        for head in range(heads):
            at = head * HEAD_DIM
            cols = [slice(part * width + at, part * width + at + HEAD_DIM) for part in range(3)]
            queries = qkvb[low:high, cols[0]]
            key_rows = qkvb[key_low:high, cols[1]]
            value_rows = qkvb[key_low:high, cols[2]]
            weights, inverse = score_block(queries, key_rows, keep)
            probs = weights * inverse
            probs_bf = probs.astype(BF16)
            mixed = dot_nn(probs_bf, value_rows)
            att[low:high, at : at + HEAD_DIM] = mixed.astype(BF16)
            d_mixed = d_attended[:, at : at + HEAD_DIM]
            d_probs = dot_nt(d_mixed, value_rows)
            delta = jnp.sum(mixed * d_mixed.astype(F32), axis=-1, keepdims=True)
            d_scores = (probs * (d_probs - delta) * HEAD_DIM ** (-0.5)).astype(BF16)
            dqkv[low:high, cols[0]] = dot_nn(d_scores, key_rows).astype(BF16)
            d_keys = dot_tn(d_scores, queries)
            d_values = dot_tn(probs_bf, d_mixed)
            if block > 0:
                past_keys, past_values = carried[head]
                dqkv[key_low:low, cols[1]] = (past_keys + d_keys[:MOST]).astype(BF16)
                dqkv[key_low:low, cols[2]] = (past_values + d_values[:MOST]).astype(BF16)
                d_keys, d_values = d_keys[MOST:], d_values[MOST:]
            if block == blocks - 1:
                dqkv[low:high, cols[1]] = d_keys.astype(BF16)
                dqkv[low:high, cols[2]] = d_values.astype(BF16)
            carried[head] = (d_keys, d_values)
        if block == 0:
            pass_on(FWD, middle[0])
    grad_copy = pltpu.make_async_remote_copy(
        src_ref=grad_out,
        dst_ref=grad_ref,
        send_sem=grad_sems.at[0],
        recv_sem=grad_sems.at[1],
        device_id=(pipes - 1 - p, t),
        device_id_type=MESH,
    )
    early = always

    def start_grad(condition):
        @pl.when(condition)
        def start():
            grad_copy.start()

    tile = 512
    for low in range(0, wide, tile):
        grad_out[:, low : low + tile] = dot_tn(att[...], c_ref[:, low : low + tile]).astype(BF16)
    start_grad(early)

    @pl.when(sends)
    def input_terms():
        for block in range(blocks):
            low, high = block * MOST, (block + 1) * MOST
            d_normed = dot_nt(dqkv[low:high, :], wb[...]) * gain_b
            widened = xb[low:high, :].astype(F32)
            scale = scales[block]
            pull = jnp.mean(d_normed * widened, axis=-1, keepdims=True) * scale * scale * scale
            term[BWD, low:high, :] = (d_normed * scale - widened * pull).astype(BF16)
        start_edges(BWD, range(1, peers))
        start_grad(jnp.logical_not(early))

    for step in middle[1:]:
        pass_on(FWD, step)
    if lent:
        pl.when(helps)(carry_for_lenders)
    pass_on(BWD, middle[0])
    finish(FWD)
    for step in middle[1:]:
        pass_on(BWD, step)

    finish(BWD)
    grad_copy.wait_recv()

    @pl.when(takes)
    def forward_landed():
        if lent:

            @pl.when(helps)
            def whole():
                for part, span in enumerate(spans(FWD, share)):
                    own_copy(FWD, span, part).wait_recv()

            @pl.when(sends)
            def both():
                for part, span in enumerate(spans(FWD, kept)):
                    own_copy(FWD, span, part).wait_recv()
                back_copy(0).wait_recv()

        else:
            own_copy(FWD, (0, share), 0).wait_recv()

    @pl.when(takes)
    def backward_landed():
        for part, span in enumerate(spans(BWD, share)):
            own_copy(BWD, span, part).wait_recv()

    grad_copy.wait_send()
    for way in (FWD, BWD):
        for member, count in classes[way]:

            @pl.when(member)
            def own_left():
                for part, span in enumerate(spans(way, count)):
                    own_copy(way, span, part).wait_send()

    if lent:

        @pl.when(lends)
        def lent_left():
            for owner in range(peers):
                lent_copy(p, owner).wait_send()

        @pl.when(helps)
        def back_left():
            for lender in range(lenders):
                back_copy(lender).wait_send()

    for flow in (RIGHT, LEFT):
        for way in (FWD, BWD):
            groups = [(member, count, False) for member, count in classes[way]]
            if lent:
                groups.append((helps, helper_count, True))
            for member, count, aid in groups:
                for step in range(1, peers):

                    @pl.when(member & (places[flow] < step))
                    def gone():
                        owner = owner_at(flow, step)
                        for part, span in enumerate(spans(way, count, aid)):
                            chain_copy(flow, way, step, owner, span, part, aid).wait_send()


HBM_SPEC = pl.BlockSpec(memory_space=pltpu.HBM)
VMEM_SPEC = pl.BlockSpec(memory_space=pltpu.VMEM)


def results_kernel(
    moved_ref, moved_grad_ref, mirrored_ref, out_hbm, out_grad_hbm, weight_hbm, wide_ref, sems
):
    copies = [
        pltpu.make_async_copy(moved_ref, out_hbm.at[0], sems.at[0]),
        pltpu.make_async_copy(moved_grad_ref, out_grad_hbm.at[0], sems.at[1]),
    ]
    for copy in copies:
        copy.start()
    parts = sems.shape[0] - 2
    size = wide_ref.shape[0] // parts
    for part in range(parts):
        at = slice(part * size, (part + 1) * size)
        wide_ref[at, :] = mirrored_ref[at, :].astype(F32)
        copy = pltpu.make_async_copy(wide_ref.at[at], weight_hbm.at[0, at], sems.at[2 + part])
        copy.start()
        copies.append(copy)
    for copy in copies:
        copy.wait()


def results_of(moved, moved_grad, mirrored):
    share, wide = moved.shape
    width = mirrored.shape[0]
    parts = 4
    return pl.pallas_call(
        results_kernel,
        out_shape=(
            jax.ShapeDtypeStruct((1, share, wide), BF16),
            jax.ShapeDtypeStruct((1, share, wide), BF16),
            jax.ShapeDtypeStruct((1, width, wide), F32),
        ),
        in_specs=[VMEM_SPEC] * 3,
        out_specs=(HBM_SPEC,) * 3,
        scratch_shapes=[pltpu.VMEM((width, wide), F32), pltpu.SemaphoreType.DMA((2 + parts,))],
        compiler_params=pltpu.CompilerParams(vmem_limit_bytes=8 * 1024 * 1024),
        name="results",
    )(moved, moved_grad, mirrored)


def per_device(
    fwd_inputs,
    bwd_inputs,
    bwd_cotangent,
    fwd_lengths,
    bwd_lengths,
    norm_gains,
    query_weight,
    key_weight,
    value_weight,
    out_weight,
):
    pipes, peers = lax.axis_size("pipe"), lax.axis_size("tensor")
    rows, wide = fwd_inputs.shape[1:]
    width = query_weight.shape[3]
    share = rows // peers
    pieces = 3
    lent = lent_rows(pipes, peers, share)
    lenders = pipes - 2 if lent else 1
    helper_count = max((lenders + 1) // 2 * lent, 16)
    dma = pltpu.SemaphoreType.DMA
    moved, moved_grad, mirrored = pl.pallas_call(
        functools.partial(sections_kernel, pipes, peers, lent),
        out_shape=(
            pltpu.VMEM((share, wide), BF16),
            pltpu.VMEM((share, wide), BF16),
            pltpu.VMEM((width, wide), BF16),
        ),
        in_specs=[HBM_SPEC] * 10,
        out_specs=(VMEM_SPEC,) * 3,
        scratch_shapes=[
            pltpu.SMEM(fwd_lengths.shape, jnp.int32),
            pltpu.SMEM(bwd_lengths.shape, jnp.int32),
            pltpu.VMEM((2, wide), BF16),
            pltpu.VMEM((rows, wide), BF16),
            pltpu.VMEM((rows, wide), BF16),
            pltpu.VMEM((rows, wide), BF16),
            pltpu.VMEM((wide, 3 * width), BF16),
            pltpu.VMEM((wide, 3 * width), BF16),
            pltpu.VMEM((width, wide), BF16),
            pltpu.VMEM((width, wide), BF16),
            pltpu.VMEM((rows + MOST, 3 * width), BF16),
            pltpu.VMEM((rows, 3 * width), BF16),
            pltpu.VMEM((rows, 3 * width), BF16),
            pltpu.VMEM((rows, width), BF16),
            pltpu.VMEM((2, rows, wide), BF16),
            pltpu.VMEM((2, share, wide), BF16),
            pltpu.VMEM((width, wide), BF16),
            pltpu.VMEM((2, 2, peers - 2, share, wide), BF16),
            pltpu.VMEM((2, 2, share, wide), BF16),
            pltpu.VMEM((2, 2, helper_count, wide), BF16),
            dma((16,)),
            dma((2, 2, peers - 1, pieces)),
            dma((2, 2, peers - 1, pieces)),
            dma((2, pieces)),
            dma((2, pieces)),
            dma((2,)),
            dma((2, 2, pieces)),
            dma((peers,)),
            dma((lenders, peers)),
            dma((lenders,)),
            dma,
        ],
        compiler_params=pltpu.CompilerParams(
            collective_id=0, has_side_effects=True, vmem_limit_bytes=VMEM_LIMIT
        ),
        cost_estimate=pl.CostEstimate(
            flops=28 * rows * wide * width,
            bytes_accessed=16 * wide * (rows + width),
            transcendentals=2 * rows * MOST,
        ),
        name="sections",
    )(
        fwd_lengths,
        bwd_lengths,
        norm_gains.reshape(2, wide),
        fwd_inputs,
        bwd_inputs,
        bwd_cotangent,
        query_weight,
        key_weight,
        value_weight,
        out_weight,
    )
    return results_of(moved, moved_grad, mirrored)


def solution(mesh):
    placed = (
        P("pipe", None, None),
        P("pipe", None, None),
        P("pipe", None, None),
        P("pipe", None),
        P("pipe", None),
        P(None, "pipe", None),
        P(None, "pipe", None, "tensor"),
        P(None, "pipe", None, "tensor"),
        P(None, "pipe", None, "tensor"),
        P(None, "pipe", "tensor", None),
    )
    return jax.shard_map(
        per_device,
        mesh=mesh,
        in_specs=placed,
        out_specs=(P("pipe", "tensor", None), P("pipe", "tensor", None), P("pipe", "tensor", None)),
        check_vma=False,
    )
```

```python
import functools

import jax
import jax.numpy as jnp
from jax import lax
from jax.experimental import pallas as pl
from jax.experimental.pallas import tpu as pltpu
from jax.sharding import PartitionSpec as P

HEAD_DIM = 128
MOST = 192
VMEM_LIMIT = 54 * 1024 * 1024
MESH = pl.DeviceIdType.MESH
RIGHT, LEFT = 0, 1
FWD, BWD = 0, 1
F32 = jnp.float32
BF16 = jnp.bfloat16


def doc_start(lengths_ref, first_row, row_count):
    position = lax.broadcasted_iota(jnp.int32, (row_count, 1), 0) + first_row
    start = jnp.zeros((row_count, 1), jnp.int32)
    end = jnp.int32(0)
    for doc in range(lengths_ref.shape[1]):
        end = end + lengths_ref[0, doc]
        start = jnp.where(position >= end, end, start)
    return position, start


def window_mask(lengths_ref, first_row, row_count, first_key, key_count):
    position, start = doc_start(lengths_ref, first_row, row_count)
    keys = lax.broadcasted_iota(jnp.int32, (row_count, key_count), 1) + first_key
    return (keys >= start) & (keys <= position)


def dot_nn(left, right):
    return jnp.dot(left, right, preferred_element_type=F32)


def dot_nt(left, right):
    return lax.dot_general(left, right, (((1,), (1,)), ((), ())), preferred_element_type=F32)


def dot_tn(left, right):
    return lax.dot_general(left, right, (((0,), (0,)), ((), ())), preferred_element_type=F32)


def normed_rows(x, gain):
    widened = x.astype(F32)
    mean_square = jnp.mean(widened * widened, axis=-1, keepdims=True)
    scale = lax.rsqrt(mean_square + 1e-05)
    return (widened * scale * gain).astype(BF16), scale


def score_block(queries, key_rows, keep):
    scores = dot_nt(queries, key_rows) * HEAD_DIM ** (-0.5)
    scores = jnp.where(keep, scores, -1e30)
    weights = jnp.exp(scores - jnp.max(scores, axis=-1, keepdims=True))
    return weights, 1.0 / jnp.sum(weights, axis=-1, keepdims=True)


def rows_at(first, count):
    return pl.ds(pl.multiple_of(first, 16), count)


def lent_rows(pipes, peers, share):
    half = (pipes - 1) // 2
    return 32 if pipes > 2 and share > 64 and half * 32 <= share else 0


def sections_kernel(
    pipes, peers, lent,
    len_f_hbm, len_b_hbm, gain_hbm, xf_hbm, xb_hbm, c_hbm, wq_hbm, wk_hbm, wv_hbm, wo_hbm,
    outf_ref, outb_ref, grad_ref,
    lens_f, lens_b, gain_ref, xf, xb, c_ref, wf, wb, wof, wob, qkvf, qkvb, dqkv, att,
    term, own, grad_out, mid_recv, last_recv, help_recv,
    load_sem, chain_send, chain_recv, own_send_sem, own_recv_sem, grad_sems,
    help_sem, lent_send, lent_recv, back_send, back_recv,
):
    p = lax.axis_index("pipe")
    t = lax.axis_index("tensor")
    rows, wide = xf.shape
    width = wof.shape[0]
    heads = width // HEAD_DIM
    share = rows // peers
    blocks = rows // MOST
    last = peers - 1
    helper = pipes - 1
    lenders = pipes - 2 if lent else 0
    half = (lenders + 1) // 2
    kept = share - lent
    sends = p < helper
    takes = p > 0
    helps = p == helper
    lends = p < lenders

    if lent:
        classes = {
            FWD: [(lends, kept), (p == lenders, share)],
            BWD: [(sends, share)],
        }
    else:
        classes = {FWD: [(sends, share)], BWD: [(sends, share)]}
    helper_count = half * lent
    inputs = (xf, c_ref)

    slot = iter(range(load_sem.shape[0]))

    def load(source, target):
        return pltpu.make_async_copy(source, target, load_sem.at[next(slot)])

    low_half = t < peers // 2
    order = [jnp.where(low_half, blocks - 1 - i, i) for i in range(blocks)]
    pair_low = jnp.where(low_half, (blocks - 2) * MOST, 0)

    gain_copy = load(gain_hbm, gain_ref)
    lens_f_copy = load(len_f_hbm, lens_f)
    pair_at, third_at = rows_at(pair_low, 2 * MOST), rows_at(order[2] * MOST, MOST)
    x_copies = [load(xf_hbm.at[0, at], xf.at[at]) for at in (pair_at, third_at)]
    wf_copies = [
        load(source.at[0, 0], wf.at[:, part * width : (part + 1) * width])
        for part, source in enumerate((wq_hbm, wk_hbm, wv_hbm))
    ]
    wof_copy = load(wo_hbm.at[0, 0], wof)
    xb_copy = load(xb_hbm.at[0], xb)
    wb_copies = [
        load(source.at[1, 0], wb.at[:, part * width : (part + 1) * width])
        for part, source in enumerate((wq_hbm, wk_hbm, wv_hbm))
    ]
    c_copy = load(c_hbm.at[0], c_ref)
    wob_copy = load(wo_hbm.at[1, 0], wob)
    lens_b_copy = load(len_b_hbm, lens_b)

    gain_copy.start()

    @pl.when(sends)
    def load_forward():
        for copy in (x_copies[0], wf_copies[1], wf_copies[0], wf_copies[2], lens_f_copy, wof_copy):
            copy.start()
        x_copies[1].start()

    barrier = pltpu.get_barrier_semaphore()
    to_right, to_left = t < last, t > 0
    chains = p >= 0 if lent else sends
    always = p >= 0
    roles = [
        (chains & to_right, chains & to_left, (p, t - 1)),
        (chains & to_left, chains & to_right, (p, t + 1)),
        (sends, takes, (p - 1, t)),
        (always, always, (helper - p, t)),
    ]
    for lender in range(lenders):
        roles.append((p == lender, helps, (lender, t)))
        roles.append((helps, p == lender + 1, (helper, t)))

    for unused, has_source, source in roles:

        @pl.when(has_source)
        def greet():
            pl.semaphore_signal(barrier, inc=1, device_id=source, device_id_type=MESH)

    def await_barrier():
        count = jnp.int32(0)
        for has_target, unused, unused_too in roles:
            count = count + has_target.astype(jnp.int32)
        pl.semaphore_wait(barrier, count)

    places = (t, last - t)

    def owner_at(flow, step):
        owner = peers - step + places[flow]
        return owner if flow == RIGHT else last - owner

    def spans(way, count, aid=False):
        if aid:
            return [(at, lent) for at in range(0, count, lent)]
        if share <= 64:
            return [(0, count)]
        if way == FWD:
            return [(0, 64), (64, count - 64)]
        tail = (48, 16)
        return [(0, count - sum(tail)), (count - sum(tail), tail[0]), (count - tail[1], tail[1])]

    def chain_copy(flow, way, step, owner, span, part=0, aid=False):
        toward = t + 1 if flow == RIGHT else t - 1
        first, size = span
        recv_sem = chain_recv.at[flow, way, step - 1, part]
        if step < last:
            target = mid_recv.at[flow, way, step - 1, first : first + size]
        elif aid:
            target = help_recv.at[flow, way, first : first + size]
            recv_sem = help_sem.at[flow, way, part]
        else:
            target = last_recv.at[flow, way, first : first + size]
        return pltpu.make_async_remote_copy(
            src_ref=term.at[way, rows_at(owner * share + first, size)],
            dst_ref=target,
            send_sem=chain_send.at[flow, way, step - 1, part],
            recv_sem=recv_sem,
            device_id=(p, toward),
            device_id_type=MESH,
        )

    def start_edges(way, steps, only=None):
        for flow in (RIGHT, LEFT):
            for member, count in classes[way]:
                parts = range(len(spans(way, count))) if only is None else only
                parts = [part for part in parts if part < len(spans(way, count))]

                @pl.when(member & (places[flow] == 0))
                def start():
                    for step in steps:
                        owner = peers - step if flow == RIGHT else step - 1
                        for part in parts:
                            span = spans(way, count)[part]
                            chain_copy(flow, way, step, owner, span, part).start()

    def pass_part(flow, way, step, span, part, aid=False):
        owner = owner_at(flow, step)
        first, size = span
        chain_copy(flow, way, step - 1, owner, span, part, aid).wait_recv()
        at = rows_at(owner * share + first, size)
        arrived = mid_recv[flow, way, step - 2, first : first + size, :]
        total = term[way, at, :].astype(F32) + arrived.astype(F32)
        term[way, at, :] = total.astype(BF16)
        chain_copy(flow, way, step, owner, span, part, aid).start()

    turns = ((LEFT, low_half), (RIGHT, always), (LEFT, jnp.logical_not(low_half)))

    def pass_on(way, step):
        for flow, turn in turns:
            here = places[flow]
            for member, count in classes[way]:

                @pl.when(member & turn & (here >= 1) & (here < step))
                def add():
                    for part, span in enumerate(spans(way, count)):
                        pass_part(flow, way, step, span, part)

    def own_copy(way, span, part):
        at = slice(span[0], span[0] + span[1])
        return pltpu.make_async_remote_copy(
            src_ref=own.at[way, at],
            dst_ref=(outf_ref, outb_ref)[way].at[at],
            send_sem=own_send_sem.at[way, part],
            recv_sem=own_recv_sem.at[way, part],
            device_id=(p + 1, t),
            device_id_type=MESH,
        )

    def finish(way):
        for member, count in classes[way]:

            @pl.when(member)
            def sum_up():
                for part, span in enumerate(spans(way, count)):
                    first, size = span
                    for flow in (RIGHT, LEFT):

                        @pl.when(places[flow] >= 1)
                        def arrive():
                            chain_copy(flow, way, last, t, span, part).wait_recv()

                    at = slice(first, first + size)
                    here = rows_at(t * share + first, size)
                    total = inputs[way][here, :].astype(F32) + term[way, here, :].astype(F32)
                    for flow in (RIGHT, LEFT):
                        total = total + last_recv[flow, way, at].astype(F32)
                    own[way, at, :] = total.astype(BF16)
                    own_copy(way, span, part).start()

    def lent_copy(lender, owner):
        to_way, place = lender // max(half, 1), lax.rem(lender, max(half, 1))
        return pltpu.make_async_remote_copy(
            src_ref=term.at[FWD, rows_at(owner * share + kept, lent)],
            dst_ref=term.at[to_way, rows_at(owner * share + place * lent, lent)],
            send_sem=lent_send.at[owner],
            recv_sem=lent_recv.at[lender, owner],
            device_id=(helper, t),
            device_id_type=MESH,
        )

    def lend(owner):
        @pl.when(lends & (owner == t))
        def own_input():
            at = rows_at(t * share + kept, lent)
            total = xf[at, :].astype(F32) + term[FWD, at, :].astype(F32)
            term[FWD, at, :] = total.astype(BF16)

        @pl.when(lends)
        def hand_over():
            lent_copy(p, owner).start()

    def back_copy(lender):
        way, place = lender // half, lender % half
        return pltpu.make_async_remote_copy(
            src_ref=own.at[way, place * lent : (place + 1) * lent],
            dst_ref=outf_ref.at[kept:share],
            send_sem=back_send.at[lender],
            recv_sem=back_recv,
            device_id=(lender + 1, t),
            device_id_type=MESH,
        )

    def carry_for_lenders():
        jobs = [
            (lender, lender // half, lender % half, (lender % half * lent, lent))
            for lender in range(lenders)
        ]

        def start_edge(way, step, span, part):
            for flow in (RIGHT, LEFT):

                @pl.when(places[flow] == 0)
                def start():
                    owner = peers - step if flow == RIGHT else step - 1
                    chain_copy(flow, way, step, owner, span, part, True).start()

        for lender, way, part, span in jobs:
            for owner in range(peers):
                lent_copy(lender, owner).wait_recv()
            start_edge(way, 1, span, part)
        for step in range(2, peers):
            for unused, way, part, span in jobs:
                start_edge(way, step, span, part)
            for flow, turn in turns:

                @pl.when(turn & (places[flow] >= 1) & (places[flow] < step))
                def add():
                    for unused, way, part, span in jobs:
                        pass_part(flow, way, step, span, part, True)

        for lender, way, part, span in jobs:
            for flow in (RIGHT, LEFT):

                @pl.when(places[flow] >= 1)
                def arrive():
                    chain_copy(flow, way, last, t, span, part, True).wait_recv()

            at = slice(span[0], span[0] + lent)
            total = term[way, rows_at(t * share + span[0], lent), :].astype(F32)
            for flow in (RIGHT, LEFT):
                total = total + help_recv[flow, way, at].astype(F32)
            own[way, at, :] = total.astype(BF16)
            back_copy(lender).start()

    qkvf[0:MOST, :] = jnp.zeros((MOST, 3 * width), BF16)
    gain_copy.wait()
    gain_f = gain_ref[0:1, :].astype(F32)
    gain_b = gain_ref[1:2, :].astype(F32)

    def attend_forward(low, count):
        window = -(-(count + MOST - 1) // 128) * 128
        first_key = jnp.maximum(low + count - window, -MOST)
        query_at = rows_at(low + MOST, count)
        key_at = rows_at(first_key + MOST, window)
        keep = window_mask(lens_f, low, count, first_key, window)
        parts = []
        for head in range(heads):
            at = head * HEAD_DIM
            weights, inverse = score_block(
                qkvf[query_at, at : at + HEAD_DIM],
                qkvf[key_at, width + at : width + at + HEAD_DIM],
                keep,
            )
            mixed = dot_nn(
                (weights * inverse).astype(BF16),
                qkvf[key_at, 2 * width + at : 2 * width + at + HEAD_DIM],
            )
            parts.append(mixed.astype(BF16))
        attended = jnp.concatenate(parts, axis=1)
        term[FWD, rows_at(low, count), :] = dot_nn(attended, wof[...]).astype(BF16)

    def load_backward():
        for copy in (xb_copy, *wb_copies, lens_b_copy, c_copy, wob_copy):
            copy.start()

    @pl.when(sends)
    def forward_first():
        x_copies[0].wait()
        normed, unused = normed_rows(xf[pair_at, :], gain_f)
        for part in (1, 0, 2):
            cols = slice(part * width, (part + 1) * width)
            wf_copies[part].wait()
            qkvf[rows_at(pair_low + MOST, 2 * MOST), cols] = dot_nn(normed, wf[:, cols]).astype(BF16)
        lens_f_copy.wait()
        wof_copy.wait()

    def first_attention(low, count):
        @pl.when(sends)
        def attend():
            attend_forward(low, count)

    by_owner = share > 64
    if by_owner:
        turn = [jnp.where(low_half, last - i, i) for i in range(peers)]
        first_attention(turn[0] * share, 64)
    else:
        first_attention(order[0] * MOST, MOST)
    await_barrier()
    start_edges(FWD, [1], [0])
    if by_owner:
        first_attention(turn[0] * share + 64, share - 64)
        start_edges(FWD, [1], [1])
        if lent:
            lend(turn[0])
    load_backward()

    @pl.when(sends)
    def project_rest():
        x_copies[1].wait()
        normed, unused = normed_rows(xf[third_at, :], gain_f)
        qkvf[rows_at((order[2] + 1) * MOST, MOST), :] = dot_nn(normed, wf[...]).astype(BF16)

    if by_owner:
        for i in range(1, peers):
            first_attention(turn[i] * share, share)
            if i < last:
                start_edges(FWD, [i + 1])
            if lent:
                lend(turn[i])
    else:
        for i in range(1, blocks):
            first_attention(order[i] * MOST, MOST)
        start_edges(FWD, range(2, peers))

    zeros = jnp.zeros((share, wide), BF16)

    @pl.when(jnp.logical_not(takes))
    def clear_results():
        outf_ref[...] = zeros
        outb_ref[...] = zeros

    for flow in (RIGHT, LEFT):

        @pl.when(places[flow] == 0)
        def clear_last():
            for way in (FWD, BWD):
                last_recv[flow, way] = zeros
                if lent:
                    help_recv[flow, way] = jnp.zeros((helper_count, wide), BF16)

    xb_copy.wait()
    scales = []
    for block in range(blocks):
        low, high = block * MOST, (block + 1) * MOST
        normed, scale = normed_rows(xb[low:high, :], gain_b)
        scales.append(scale)
        if block == 0:
            for copy in wb_copies:
                copy.wait()
        qkvb[low:high, :] = dot_nn(normed, wb[...]).astype(BF16)
    c_copy.wait()
    wob_copy.wait()
    lens_b_copy.wait()
    middle = [step for step in range(2, peers)]
    carried = {}
    for block in range(blocks):
        low, high = block * MOST, (block + 1) * MOST
        key_low = max(0, low - MOST)
        keep = window_mask(lens_b, low, MOST, key_low, high - key_low)
        d_attended = dot_nt(c_ref[low:high, :], wob[...]).astype(BF16)
        for head in range(heads):
            at = head * HEAD_DIM
            cols = [slice(part * width + at, part * width + at + HEAD_DIM) for part in range(3)]
            queries = qkvb[low:high, cols[0]]
            key_rows = qkvb[key_low:high, cols[1]]
            value_rows = qkvb[key_low:high, cols[2]]
            weights, inverse = score_block(queries, key_rows, keep)
            probs = weights * inverse
            probs_bf = probs.astype(BF16)
            mixed = dot_nn(probs_bf, value_rows)
            att[low:high, at : at + HEAD_DIM] = mixed.astype(BF16)
            d_mixed = d_attended[:, at : at + HEAD_DIM]
            d_probs = dot_nt(d_mixed, value_rows)
            delta = jnp.sum(mixed * d_mixed.astype(F32), axis=-1, keepdims=True)
            d_scores = (probs * (d_probs - delta) * HEAD_DIM ** (-0.5)).astype(BF16)
            dqkv[low:high, cols[0]] = dot_nn(d_scores, key_rows).astype(BF16)
            d_keys = dot_tn(d_scores, queries)
            d_values = dot_tn(probs_bf, d_mixed)
            if block > 0:
                past_keys, past_values = carried[head]
                dqkv[key_low:low, cols[1]] = (past_keys + d_keys[:MOST]).astype(BF16)
                dqkv[key_low:low, cols[2]] = (past_values + d_values[:MOST]).astype(BF16)
                d_keys, d_values = d_keys[MOST:], d_values[MOST:]
            if block == blocks - 1:
                dqkv[low:high, cols[1]] = d_keys.astype(BF16)
                dqkv[low:high, cols[2]] = d_values.astype(BF16)
            carried[head] = (d_keys, d_values)
        if block == 0:
            pass_on(FWD, middle[0])
    grad_copy = pltpu.make_async_remote_copy(
        src_ref=grad_out,
        dst_ref=grad_ref,
        send_sem=grad_sems.at[0],
        recv_sem=grad_sems.at[1],
        device_id=(pipes - 1 - p, t),
        device_id_type=MESH,
    )
    early = always

    def start_grad(condition):
        @pl.when(condition)
        def start():
            grad_copy.start()

    tile = 512
    for low in range(0, wide, tile):
        grad_out[:, low : low + tile] = dot_tn(att[...], c_ref[:, low : low + tile]).astype(BF16)
    start_grad(early)

    @pl.when(sends)
    def input_terms():
        for block in range(blocks):
            low, high = block * MOST, (block + 1) * MOST
            d_normed = dot_nt(dqkv[low:high, :], wb[...]) * gain_b
            widened = xb[low:high, :].astype(F32)
            scale = scales[block]
            pull = jnp.mean(d_normed * widened, axis=-1, keepdims=True) * scale * scale * scale
            term[BWD, low:high, :] = (d_normed * scale - widened * pull).astype(BF16)
        start_edges(BWD, range(1, peers))
        start_grad(jnp.logical_not(early))

    for step in middle[1:]:
        pass_on(FWD, step)
    if lent:
        pl.when(helps)(carry_for_lenders)
    pass_on(BWD, middle[0])
    finish(FWD)
    for step in middle[1:]:
        pass_on(BWD, step)

    def gone(way, steps):
        for flow in (RIGHT, LEFT):
            for member, count in classes[way]:
                for step in steps:

                    @pl.when(member & (places[flow] < step))
                    def chain_gone():
                        owner = owner_at(flow, step)
                        for part, span in enumerate(spans(way, count)):
                            chain_copy(flow, way, step, owner, span, part).wait_send()

    def own_gone(way):
        for member, count in classes[way]:

            @pl.when(member)
            def sum_gone():
                for part, span in enumerate(spans(way, count)):
                    own_copy(way, span, part).wait_send()

    gone(FWD, range(1, peers))
    own_gone(FWD)
    if lent:

        @pl.when(lends)
        def lent_gone():
            for owner in range(peers):
                lent_copy(p, owner).wait_send()

        @pl.when(helps)
        def help_gone():
            for flow in (RIGHT, LEFT):
                for step in range(1, peers):

                    @pl.when(places[flow] < step)
                    def chain_gone():
                        owner = owner_at(flow, step)
                        for way in (FWD, BWD):
                            for part, span in enumerate(spans(way, helper_count, True)):
                                chain_copy(flow, way, step, owner, span, part, True).wait_send()

            for lender in range(lenders):
                back_copy(lender).wait_send()

    grad_copy.wait_recv()
    grad_copy.wait_send()
    gone(BWD, range(1, last))
    finish(BWD)

    @pl.when(takes)
    def forward_landed():
        if lent:

            @pl.when(helps)
            def whole():
                for part, span in enumerate(spans(FWD, share)):
                    own_copy(FWD, span, part).wait_recv()

            @pl.when(sends)
            def both():
                for part, span in enumerate(spans(FWD, kept)):
                    own_copy(FWD, span, part).wait_recv()
                back_copy(0).wait_recv()

        else:
            own_copy(FWD, (0, share), 0).wait_recv()

    gone(BWD, [last])
    own_gone(BWD)

    @pl.when(takes)
    def backward_landed():
        for part, span in enumerate(spans(BWD, share)):
            own_copy(BWD, span, part).wait_recv()


HBM_SPEC = pl.BlockSpec(memory_space=pltpu.HBM)
VMEM_SPEC = pl.BlockSpec(memory_space=pltpu.VMEM)


def results_kernel(
    moved_ref, moved_grad_ref, mirrored_ref, out_hbm, out_grad_hbm, weight_hbm, wide_ref, sems
):
    copies = [
        pltpu.make_async_copy(moved_ref, out_hbm.at[0], sems.at[0]),
        pltpu.make_async_copy(moved_grad_ref, out_grad_hbm.at[0], sems.at[1]),
    ]
    for copy in copies:
        copy.start()
    parts = sems.shape[0] - 2
    size = wide_ref.shape[0] // parts
    for part in range(parts):
        at = slice(part * size, (part + 1) * size)
        wide_ref[at, :] = mirrored_ref[at, :].astype(F32)
        copy = pltpu.make_async_copy(wide_ref.at[at], weight_hbm.at[0, at], sems.at[2 + part])
        copy.start()
        copies.append(copy)
    for copy in copies:
        copy.wait()


def results_of(moved, moved_grad, mirrored):
    share, wide = moved.shape
    width = mirrored.shape[0]
    parts = 4
    return pl.pallas_call(
        results_kernel,
        out_shape=(
            jax.ShapeDtypeStruct((1, share, wide), BF16),
            jax.ShapeDtypeStruct((1, share, wide), BF16),
            jax.ShapeDtypeStruct((1, width, wide), F32),
        ),
        in_specs=[VMEM_SPEC] * 3,
        out_specs=(HBM_SPEC,) * 3,
        scratch_shapes=[pltpu.VMEM((width, wide), F32), pltpu.SemaphoreType.DMA((2 + parts,))],
        compiler_params=pltpu.CompilerParams(vmem_limit_bytes=8 * 1024 * 1024),
        name="results",
    )(moved, moved_grad, mirrored)


def per_device(
    fwd_inputs,
    bwd_inputs,
    bwd_cotangent,
    fwd_lengths,
    bwd_lengths,
    norm_gains,
    query_weight,
    key_weight,
    value_weight,
    out_weight,
):
    pipes, peers = lax.axis_size("pipe"), lax.axis_size("tensor")
    rows, wide = fwd_inputs.shape[1:]
    width = query_weight.shape[3]
    share = rows // peers
    pieces = 3
    lent = lent_rows(pipes, peers, share)
    lenders = pipes - 2 if lent else 1
    helper_count = max((lenders + 1) // 2 * lent, 16)
    dma = pltpu.SemaphoreType.DMA
    moved, moved_grad, mirrored = pl.pallas_call(
        functools.partial(sections_kernel, pipes, peers, lent),
        out_shape=(
            pltpu.VMEM((share, wide), BF16),
            pltpu.VMEM((share, wide), BF16),
            pltpu.VMEM((width, wide), BF16),
        ),
        in_specs=[HBM_SPEC] * 10,
        out_specs=(VMEM_SPEC,) * 3,
        scratch_shapes=[
            pltpu.SMEM(fwd_lengths.shape, jnp.int32),
            pltpu.SMEM(bwd_lengths.shape, jnp.int32),
            pltpu.VMEM((2, wide), BF16),
            pltpu.VMEM((rows, wide), BF16),
            pltpu.VMEM((rows, wide), BF16),
            pltpu.VMEM((rows, wide), BF16),
            pltpu.VMEM((wide, 3 * width), BF16),
            pltpu.VMEM((wide, 3 * width), BF16),
            pltpu.VMEM((width, wide), BF16),
            pltpu.VMEM((width, wide), BF16),
            pltpu.VMEM((rows + MOST, 3 * width), BF16),
            pltpu.VMEM((rows, 3 * width), BF16),
            pltpu.VMEM((rows, 3 * width), BF16),
            pltpu.VMEM((rows, width), BF16),
            pltpu.VMEM((2, rows, wide), BF16),
            pltpu.VMEM((2, share, wide), BF16),
            pltpu.VMEM((width, wide), BF16),
            pltpu.VMEM((2, 2, peers - 2, share, wide), BF16),
            pltpu.VMEM((2, 2, share, wide), BF16),
            pltpu.VMEM((2, 2, helper_count, wide), BF16),
            dma((16,)),
            dma((2, 2, peers - 1, pieces)),
            dma((2, 2, peers - 1, pieces)),
            dma((2, pieces)),
            dma((2, pieces)),
            dma((2,)),
            dma((2, 2, pieces)),
            dma((peers,)),
            dma((lenders, peers)),
            dma((lenders,)),
            dma,
        ],
        compiler_params=pltpu.CompilerParams(
            collective_id=0, has_side_effects=True, vmem_limit_bytes=VMEM_LIMIT
        ),
        cost_estimate=pl.CostEstimate(
            flops=28 * rows * wide * width,
            bytes_accessed=16 * wide * (rows + width),
            transcendentals=2 * rows * MOST,
        ),
        name="sections",
    )(
        fwd_lengths,
        bwd_lengths,
        norm_gains.reshape(2, wide),
        fwd_inputs,
        bwd_inputs,
        bwd_cotangent,
        query_weight,
        key_weight,
        value_weight,
        out_weight,
    )
    return results_of(moved, moved_grad, mirrored)


def solution(mesh):
    placed = (
        P("pipe", None, None),
        P("pipe", None, None),
        P("pipe", None, None),
        P("pipe", None),
        P("pipe", None),
        P(None, "pipe", None),
        P(None, "pipe", None, "tensor"),
        P(None, "pipe", None, "tensor"),
        P(None, "pipe", None, "tensor"),
        P(None, "pipe", "tensor", None),
    )
    return jax.shard_map(
        per_device,
        mesh=mesh,
        in_specs=placed,
        out_specs=(P("pipe", "tensor", None), P("pipe", "tensor", None), P("pipe", "tensor", None)),
        check_vma=False,
    )
```

```python
import functools

import jax
import jax.numpy as jnp
from jax import lax
from jax.experimental import pallas as pl
from jax.experimental.pallas import tpu as pltpu
from jax.sharding import PartitionSpec as P

HEAD_DIM = 128
MOST = 192
VMEM_LIMIT = 54 * 1024 * 1024
MESH = pl.DeviceIdType.MESH
RIGHT, LEFT = 0, 1
FWD, BWD = 0, 1
F32 = jnp.float32
BF16 = jnp.bfloat16


def doc_start(lengths_ref, first_row, row_count):
    position = lax.broadcasted_iota(jnp.int32, (row_count, 1), 0) + first_row
    start = jnp.zeros((row_count, 1), jnp.int32)
    end = jnp.int32(0)
    for doc in range(lengths_ref.shape[1]):
        end = end + lengths_ref[0, doc]
        start = jnp.where(position >= end, end, start)
    return position, start


def window_mask(lengths_ref, first_row, row_count, first_key, key_count):
    position, start = doc_start(lengths_ref, first_row, row_count)
    keys = lax.broadcasted_iota(jnp.int32, (row_count, key_count), 1) + first_key
    return (keys >= start) & (keys <= position)


def dot_nn(left, right):
    return jnp.dot(left, right, preferred_element_type=F32)


def dot_nt(left, right):
    return lax.dot_general(left, right, (((1,), (1,)), ((), ())), preferred_element_type=F32)


def dot_tn(left, right):
    return lax.dot_general(left, right, (((0,), (0,)), ((), ())), preferred_element_type=F32)


def normed_rows(x, gain):
    widened = x.astype(F32)
    mean_square = jnp.mean(widened * widened, axis=-1, keepdims=True)
    scale = lax.rsqrt(mean_square + 1e-05)
    return (widened * scale * gain).astype(BF16), scale


def score_block(queries, key_rows, keep):
    scores = dot_nt(queries, key_rows) * HEAD_DIM ** (-0.5)
    scores = jnp.where(keep, scores, -1e30)
    weights = jnp.exp(scores - jnp.max(scores, axis=-1, keepdims=True))
    return weights, 1.0 / jnp.sum(weights, axis=-1, keepdims=True)


def rows_at(first, count):
    return pl.ds(pl.multiple_of(first, 16), count)


def lent_rows(pipes, peers, share):
    half = (pipes - 1) // 2
    return 32 if pipes > 2 and share > 64 and half * 32 <= share else 0


def sections_kernel(
    pipes, peers, lent,
    len_f_hbm, len_b_hbm, gain_hbm, xf_hbm, xb_hbm, c_hbm, wq_hbm, wk_hbm, wv_hbm, wo_hbm,
    outf_ref, outb_ref, grad_ref,
    lens_f, lens_b, gain_ref, xf, xb, c_ref, wf, wb, wof, wob, qkvf, qkvb, dqkv, att,
    term, own, grad_out, mid_recv, last_recv, help_recv,
    load_sem, chain_send, chain_recv, own_send_sem, own_recv_sem, grad_sems,
    help_sem, lent_send, lent_recv, back_send, back_recv,
):
    p = lax.axis_index("pipe")
    t = lax.axis_index("tensor")
    rows, wide = xf.shape
    width = wof.shape[0]
    heads = width // HEAD_DIM
    share = rows // peers
    blocks = rows // MOST
    last = peers - 1
    helper = pipes - 1
    lenders = pipes - 2 if lent else 0
    half = (lenders + 1) // 2
    kept = share - lent
    sends = p < helper
    takes = p > 0
    helps = p == helper
    lends = p < lenders

    if lent:
        classes = {
            FWD: [(lends, kept), (p == lenders, share)],
            BWD: [(sends, share)],
        }
    else:
        classes = {FWD: [(sends, share)], BWD: [(sends, share)]}
    helper_count = half * lent
    inputs = (xf, c_ref)

    slot = iter(range(load_sem.shape[0]))

    def load(source, target):
        return pltpu.make_async_copy(source, target, load_sem.at[next(slot)])

    low_half = t < peers // 2
    order = [jnp.where(low_half, blocks - 1 - i, i) for i in range(blocks)]
    pair_low = jnp.where(low_half, (blocks - 2) * MOST, 0)

    gain_copy = load(gain_hbm, gain_ref)
    lens_f_copy = load(len_f_hbm, lens_f)
    pair_at, third_at = rows_at(pair_low, 2 * MOST), rows_at(order[2] * MOST, MOST)
    x_copies = [load(xf_hbm.at[0, at], xf.at[at]) for at in (pair_at, third_at)]
    wf_copies = [
        load(source.at[0, 0], wf.at[:, part * width : (part + 1) * width])
        for part, source in enumerate((wq_hbm, wk_hbm, wv_hbm))
    ]
    wof_copy = load(wo_hbm.at[0, 0], wof)
    xb_copy = load(xb_hbm.at[0], xb)
    wb_copies = [
        load(source.at[1, 0], wb.at[:, part * width : (part + 1) * width])
        for part, source in enumerate((wq_hbm, wk_hbm, wv_hbm))
    ]
    c_copy = load(c_hbm.at[0], c_ref)
    wob_copy = load(wo_hbm.at[1, 0], wob)
    lens_b_copy = load(len_b_hbm, lens_b)

    gain_copy.start()

    @pl.when(sends)
    def load_forward():
        for copy in (x_copies[0], wf_copies[1], wf_copies[0], wf_copies[2], lens_f_copy, wof_copy):
            copy.start()
        x_copies[1].start()

    barrier = pltpu.get_barrier_semaphore()
    to_right, to_left = t < last, t > 0
    chains = p >= 0 if lent else sends
    always = p >= 0
    roles = [
        (chains & to_right, chains & to_left, (p, t - 1)),
        (chains & to_left, chains & to_right, (p, t + 1)),
        (sends, takes, (p - 1, t)),
        (always, always, (helper - p, t)),
    ]
    for lender in range(lenders):
        roles.append((p == lender, helps, (lender, t)))
        roles.append((helps, p == lender + 1, (helper, t)))

    for unused, has_source, source in roles:

        @pl.when(has_source)
        def greet():
            pl.semaphore_signal(barrier, inc=1, device_id=source, device_id_type=MESH)

    def await_barrier():
        count = jnp.int32(0)
        for has_target, unused, unused_too in roles:
            count = count + has_target.astype(jnp.int32)
        pl.semaphore_wait(barrier, count)

    places = (t, last - t)

    def owner_at(flow, step):
        owner = peers - step + places[flow]
        return owner if flow == RIGHT else last - owner

    def spans(way, count, aid=False):
        if aid:
            return [(at, lent) for at in range(0, count, lent)]
        if share <= 64:
            return [(0, count)]
        if way == FWD:
            return [(0, 64), (64, count - 64)]
        tail = (48, 16)
        return [(0, count - sum(tail)), (count - sum(tail), tail[0]), (count - tail[1], tail[1])]

    def chain_copy(flow, way, step, owner, span, part=0, aid=False):
        toward = t + 1 if flow == RIGHT else t - 1
        first, size = span
        recv_sem = chain_recv.at[flow, way, step - 1, part]
        if step < last:
            target = mid_recv.at[flow, way, step - 1, first : first + size]
        elif aid:
            target = help_recv.at[flow, way, first : first + size]
            recv_sem = help_sem.at[flow, way, part]
        else:
            target = last_recv.at[flow, way, first : first + size]
        return pltpu.make_async_remote_copy(
            src_ref=term.at[way, rows_at(owner * share + first, size)],
            dst_ref=target,
            send_sem=chain_send.at[flow, way, step - 1, part],
            recv_sem=recv_sem,
            device_id=(p, toward),
            device_id_type=MESH,
        )

    def start_edges(way, steps, only=None):
        for flow in (RIGHT, LEFT):
            for member, count in classes[way]:
                parts = range(len(spans(way, count))) if only is None else only
                parts = [part for part in parts if part < len(spans(way, count))]

                @pl.when(member & (places[flow] == 0))
                def start():
                    for step in steps:
                        owner = peers - step if flow == RIGHT else step - 1
                        for part in parts:
                            span = spans(way, count)[part]
                            chain_copy(flow, way, step, owner, span, part).start()

    def pass_part(flow, way, step, span, part, aid=False):
        owner = owner_at(flow, step)
        first, size = span
        chain_copy(flow, way, step - 1, owner, span, part, aid).wait_recv()
        at = rows_at(owner * share + first, size)
        arrived = mid_recv[flow, way, step - 2, first : first + size, :]
        total = term[way, at, :].astype(F32) + arrived.astype(F32)
        term[way, at, :] = total.astype(BF16)
        chain_copy(flow, way, step, owner, span, part, aid).start()

    turns = ((LEFT, low_half), (RIGHT, always), (LEFT, jnp.logical_not(low_half)))

    def pass_on(way, step):
        for flow, turn in turns:
            here = places[flow]
            for member, count in classes[way]:

                @pl.when(member & turn & (here >= 1) & (here < step))
                def add():
                    for part, span in enumerate(spans(way, count)):
                        pass_part(flow, way, step, span, part)

    def own_copy(way, span, part):
        at = slice(span[0], span[0] + span[1])
        return pltpu.make_async_remote_copy(
            src_ref=own.at[way, at],
            dst_ref=(outf_ref, outb_ref)[way].at[at],
            send_sem=own_send_sem.at[way, part],
            recv_sem=own_recv_sem.at[way, part],
            device_id=(p + 1, t),
            device_id_type=MESH,
        )

    def finish(way):
        for member, count in classes[way]:

            @pl.when(member)
            def sum_up():
                for part, span in enumerate(spans(way, count)):
                    first, size = span
                    for flow in (RIGHT, LEFT):

                        @pl.when(places[flow] >= 1)
                        def arrive():
                            chain_copy(flow, way, last, t, span, part).wait_recv()

                    at = slice(first, first + size)
                    here = rows_at(t * share + first, size)
                    total = inputs[way][here, :].astype(F32) + term[way, here, :].astype(F32)
                    for flow in (RIGHT, LEFT):
                        total = total + last_recv[flow, way, at].astype(F32)
                    own[way, at, :] = total.astype(BF16)
                    own_copy(way, span, part).start()

    def lent_copy(lender, owner):
        to_way, place = lender // max(half, 1), lax.rem(lender, max(half, 1))
        return pltpu.make_async_remote_copy(
            src_ref=term.at[FWD, rows_at(owner * share + kept, lent)],
            dst_ref=term.at[to_way, rows_at(owner * share + place * lent, lent)],
            send_sem=lent_send.at[owner],
            recv_sem=lent_recv.at[lender, owner],
            device_id=(helper, t),
            device_id_type=MESH,
        )

    def lend(owner):
        @pl.when(lends & (owner == t))
        def own_input():
            at = rows_at(t * share + kept, lent)
            total = xf[at, :].astype(F32) + term[FWD, at, :].astype(F32)
            term[FWD, at, :] = total.astype(BF16)

        @pl.when(lends)
        def hand_over():
            lent_copy(p, owner).start()

    def back_copy(lender):
        way, place = lender // half, lender % half
        return pltpu.make_async_remote_copy(
            src_ref=own.at[way, place * lent : (place + 1) * lent],
            dst_ref=outf_ref.at[kept:share],
            send_sem=back_send.at[lender],
            recv_sem=back_recv,
            device_id=(lender + 1, t),
            device_id_type=MESH,
        )

    def carry_for_lenders():
        jobs = [
            (lender, lender // half, lender % half, (lender % half * lent, lent))
            for lender in range(lenders)
        ]

        def start_edge(way, step, span, part):
            for flow in (RIGHT, LEFT):

                @pl.when(places[flow] == 0)
                def start():
                    owner = peers - step if flow == RIGHT else step - 1
                    chain_copy(flow, way, step, owner, span, part, True).start()

        for lender, way, part, span in jobs:
            for owner in range(peers):
                lent_copy(lender, owner).wait_recv()
            start_edge(way, 1, span, part)
        for step in range(2, peers):
            for unused, way, part, span in jobs:
                start_edge(way, step, span, part)
            for flow, turn in turns:

                @pl.when(turn & (places[flow] >= 1) & (places[flow] < step))
                def add():
                    for unused, way, part, span in jobs:
                        pass_part(flow, way, step, span, part, True)

        for lender, way, part, span in jobs:
            for flow in (RIGHT, LEFT):

                @pl.when(places[flow] >= 1)
                def arrive():
                    chain_copy(flow, way, last, t, span, part, True).wait_recv()

            at = slice(span[0], span[0] + lent)
            total = term[way, rows_at(t * share + span[0], lent), :].astype(F32)
            for flow in (RIGHT, LEFT):
                total = total + help_recv[flow, way, at].astype(F32)
            own[way, at, :] = total.astype(BF16)
            back_copy(lender).start()

    qkvf[0:MOST, :] = jnp.zeros((MOST, 3 * width), BF16)
    gain_copy.wait()
    gain_f = gain_ref[0:1, :].astype(F32)
    gain_b = gain_ref[1:2, :].astype(F32)

    def attend_forward(low, count):
        window = -(-(count + MOST - 1) // 128) * 128
        first_key = jnp.maximum(low + count - window, -MOST)
        query_at = rows_at(low + MOST, count)
        key_at = rows_at(first_key + MOST, window)
        keep = window_mask(lens_f, low, count, first_key, window)
        parts = []
        for head in range(heads):
            at = head * HEAD_DIM
            weights, inverse = score_block(
                qkvf[query_at, at : at + HEAD_DIM],
                qkvf[key_at, width + at : width + at + HEAD_DIM],
                keep,
            )
            mixed = dot_nn(
                (weights * inverse).astype(BF16),
                qkvf[key_at, 2 * width + at : 2 * width + at + HEAD_DIM],
            )
            parts.append(mixed.astype(BF16))
        attended = jnp.concatenate(parts, axis=1)
        term[FWD, rows_at(low, count), :] = dot_nn(attended, wof[...]).astype(BF16)

    def load_backward():
        for copy in (xb_copy, *wb_copies, lens_b_copy, c_copy, wob_copy):
            copy.start()

    @pl.when(sends)
    def forward_first():
        x_copies[0].wait()
        normed, unused = normed_rows(xf[pair_at, :], gain_f)
        for part in (1, 0, 2):
            cols = slice(part * width, (part + 1) * width)
            wf_copies[part].wait()
            qkvf[rows_at(pair_low + MOST, 2 * MOST), cols] = dot_nn(normed, wf[:, cols]).astype(BF16)
        lens_f_copy.wait()
        wof_copy.wait()

    def first_attention(low, count):
        @pl.when(sends)
        def attend():
            attend_forward(low, count)

    by_owner = share > 64 and share <= MOST and peers > blocks
    if by_owner:
        turn = [jnp.where(low_half, last - i, i) for i in range(peers)]
        first_attention(turn[0] * share, 64)
    else:
        first_attention(order[0] * MOST, MOST)
    await_barrier()
    start_edges(FWD, [1], [0])
    if by_owner:
        first_attention(turn[0] * share + 64, share - 64)
        start_edges(FWD, [1], [1])
        if lent:
            lend(turn[0])
    load_backward()

    @pl.when(sends)
    def project_rest():
        x_copies[1].wait()
        normed, unused = normed_rows(xf[third_at, :], gain_f)
        qkvf[rows_at((order[2] + 1) * MOST, MOST), :] = dot_nn(normed, wf[...]).astype(BF16)

    if by_owner:
        for i in range(1, peers):
            first_attention(turn[i] * share, share)
            if i < last:
                start_edges(FWD, [i + 1])
            if lent:
                lend(turn[i])
    else:
        for i in range(1, blocks):
            first_attention(order[i] * MOST, MOST)
        start_edges(FWD, range(2, peers))

    zeros = jnp.zeros((share, wide), BF16)

    @pl.when(jnp.logical_not(takes))
    def clear_results():
        outf_ref[...] = zeros
        outb_ref[...] = zeros

    for flow in (RIGHT, LEFT):

        @pl.when(places[flow] == 0)
        def clear_last():
            for way in (FWD, BWD):
                last_recv[flow, way] = zeros
                if lent:
                    help_recv[flow, way] = jnp.zeros((helper_count, wide), BF16)

    xb_copy.wait()
    for block in range(blocks):
        low, high = block * MOST, (block + 1) * MOST
        normed, unused = normed_rows(xb[low:high, :], gain_b)
        if block == 0:
            for copy in wb_copies:
                copy.wait()
        qkvb[low:high, :] = dot_nn(normed, wb[...]).astype(BF16)
    c_copy.wait()
    wob_copy.wait()
    lens_b_copy.wait()
    middle = [step for step in range(2, peers)]
    carried = {}
    for block in range(blocks):
        low, high = block * MOST, (block + 1) * MOST
        key_low = max(0, low - MOST)
        keep = window_mask(lens_b, low, MOST, key_low, high - key_low)
        d_attended = dot_nt(c_ref[low:high, :], wob[...]).astype(BF16)
        for head in range(heads):
            at = head * HEAD_DIM
            cols = [slice(part * width + at, part * width + at + HEAD_DIM) for part in range(3)]
            queries = qkvb[low:high, cols[0]]
            key_rows = qkvb[key_low:high, cols[1]]
            value_rows = qkvb[key_low:high, cols[2]]
            weights, inverse = score_block(queries, key_rows, keep)
            probs = weights * inverse
            probs_bf = probs.astype(BF16)
            mixed = dot_nn(probs_bf, value_rows)
            att[low:high, at : at + HEAD_DIM] = mixed.astype(BF16)
            d_mixed = d_attended[:, at : at + HEAD_DIM]
            d_probs = dot_nt(d_mixed, value_rows)
            delta = jnp.sum(mixed * d_mixed.astype(F32), axis=-1, keepdims=True)
            d_scores = (probs * (d_probs - delta) * HEAD_DIM ** (-0.5)).astype(BF16)
            dqkv[low:high, cols[0]] = dot_nn(d_scores, key_rows).astype(BF16)
            d_keys = dot_tn(d_scores, queries)
            d_values = dot_tn(probs_bf, d_mixed)
            if block > 0:
                past_keys, past_values = carried[head]
                dqkv[key_low:low, cols[1]] = (past_keys + d_keys[:MOST]).astype(BF16)
                dqkv[key_low:low, cols[2]] = (past_values + d_values[:MOST]).astype(BF16)
                d_keys, d_values = d_keys[MOST:], d_values[MOST:]
            if block == blocks - 1:
                dqkv[low:high, cols[1]] = d_keys.astype(BF16)
                dqkv[low:high, cols[2]] = d_values.astype(BF16)
            carried[head] = (d_keys, d_values)
        if block == 0:
            pass_on(FWD, middle[0])
    grad_copy = pltpu.make_async_remote_copy(
        src_ref=grad_out,
        dst_ref=grad_ref,
        send_sem=grad_sems.at[0],
        recv_sem=grad_sems.at[1],
        device_id=(pipes - 1 - p, t),
        device_id_type=MESH,
    )
    early = always

    def start_grad(condition):
        @pl.when(condition)
        def start():
            grad_copy.start()

    tile = 512
    for low in range(0, wide, tile):
        grad_out[:, low : low + tile] = dot_tn(att[...], c_ref[:, low : low + tile]).astype(BF16)
    start_grad(early)

    def input_terms(low):
        at = rows_at(low, MOST)
        widened = xb[at, :].astype(F32)
        scale = lax.rsqrt(jnp.mean(widened * widened, axis=-1, keepdims=True) + 1e-05)
        d_normed = dot_nt(dqkv[at, :], wb[...]) * gain_b
        pull = jnp.mean(d_normed * widened, axis=-1, keepdims=True) * scale * scale * scale
        term[BWD, at, :] = (d_normed * scale - widened * pull).astype(BF16)

    for i in range(blocks):
        pl.when(sends)(functools.partial(input_terms, order[i] * MOST))
        if by_owner and i < blocks - 1:
            start_edges(BWD, [i + 1])
    start_edges(BWD, range(blocks if by_owner else 1, peers))
    start_grad(jnp.logical_not(early))

    for step in middle[1:]:
        pass_on(FWD, step)
    if lent:
        pl.when(helps)(carry_for_lenders)
    pass_on(BWD, middle[0])
    finish(FWD)
    for step in middle[1:]:
        pass_on(BWD, step)

    def gone(way, steps):
        for flow in (RIGHT, LEFT):
            for member, count in classes[way]:
                for step in steps:

                    @pl.when(member & (places[flow] < step))
                    def chain_gone():
                        owner = owner_at(flow, step)
                        for part, span in enumerate(spans(way, count)):
                            chain_copy(flow, way, step, owner, span, part).wait_send()

    def own_gone(way):
        for member, count in classes[way]:

            @pl.when(member)
            def sum_gone():
                for part, span in enumerate(spans(way, count)):
                    own_copy(way, span, part).wait_send()

    gone(FWD, range(1, peers))
    own_gone(FWD)
    if lent:

        @pl.when(lends)
        def lent_gone():
            for owner in range(peers):
                lent_copy(p, owner).wait_send()

        @pl.when(helps)
        def help_gone():
            for flow in (RIGHT, LEFT):
                for step in range(1, peers):

                    @pl.when(places[flow] < step)
                    def chain_gone():
                        owner = owner_at(flow, step)
                        for way in (FWD, BWD):
                            for part, span in enumerate(spans(way, helper_count, True)):
                                chain_copy(flow, way, step, owner, span, part, True).wait_send()

            for lender in range(lenders):
                back_copy(lender).wait_send()

    grad_copy.wait_recv()
    grad_copy.wait_send()
    gone(BWD, range(1, last))
    finish(BWD)

    @pl.when(takes)
    def forward_landed():
        if lent:

            @pl.when(helps)
            def whole():
                for part, span in enumerate(spans(FWD, share)):
                    own_copy(FWD, span, part).wait_recv()

            @pl.when(sends)
            def both():
                for part, span in enumerate(spans(FWD, kept)):
                    own_copy(FWD, span, part).wait_recv()
                back_copy(0).wait_recv()

        else:
            own_copy(FWD, (0, share), 0).wait_recv()

    gone(BWD, [last])
    own_gone(BWD)

    @pl.when(takes)
    def backward_landed():
        for part, span in enumerate(spans(BWD, share)):
            own_copy(BWD, span, part).wait_recv()


HBM_SPEC = pl.BlockSpec(memory_space=pltpu.HBM)
VMEM_SPEC = pl.BlockSpec(memory_space=pltpu.VMEM)


def results_kernel(
    moved_ref, moved_grad_ref, mirrored_ref, out_hbm, out_grad_hbm, weight_hbm, wide_ref, sems
):
    copies = [
        pltpu.make_async_copy(moved_ref, out_hbm.at[0], sems.at[0]),
        pltpu.make_async_copy(moved_grad_ref, out_grad_hbm.at[0], sems.at[1]),
    ]
    for copy in copies:
        copy.start()
    parts = sems.shape[0] - 2
    size = wide_ref.shape[0] // parts
    for part in range(parts):
        at = slice(part * size, (part + 1) * size)
        wide_ref[at, :] = mirrored_ref[at, :].astype(F32)
        copy = pltpu.make_async_copy(wide_ref.at[at], weight_hbm.at[0, at], sems.at[2 + part])
        copy.start()
        copies.append(copy)
    for copy in copies:
        copy.wait()


def results_of(moved, moved_grad, mirrored):
    share, wide = moved.shape
    width = mirrored.shape[0]
    parts = 4
    return pl.pallas_call(
        results_kernel,
        out_shape=(
            jax.ShapeDtypeStruct((1, share, wide), BF16),
            jax.ShapeDtypeStruct((1, share, wide), BF16),
            jax.ShapeDtypeStruct((1, width, wide), F32),
        ),
        in_specs=[VMEM_SPEC] * 3,
        out_specs=(HBM_SPEC,) * 3,
        scratch_shapes=[pltpu.VMEM((width, wide), F32), pltpu.SemaphoreType.DMA((2 + parts,))],
        compiler_params=pltpu.CompilerParams(vmem_limit_bytes=8 * 1024 * 1024),
        name="results",
    )(moved, moved_grad, mirrored)


def per_device(
    fwd_inputs,
    bwd_inputs,
    bwd_cotangent,
    fwd_lengths,
    bwd_lengths,
    norm_gains,
    query_weight,
    key_weight,
    value_weight,
    out_weight,
):
    pipes, peers = lax.axis_size("pipe"), lax.axis_size("tensor")
    rows, wide = fwd_inputs.shape[1:]
    width = query_weight.shape[3]
    share = rows // peers
    pieces = 3
    lent = lent_rows(pipes, peers, share)
    lenders = pipes - 2 if lent else 1
    helper_count = max((lenders + 1) // 2 * lent, 16)
    dma = pltpu.SemaphoreType.DMA
    moved, moved_grad, mirrored = pl.pallas_call(
        functools.partial(sections_kernel, pipes, peers, lent),
        out_shape=(
            pltpu.VMEM((share, wide), BF16),
            pltpu.VMEM((share, wide), BF16),
            pltpu.VMEM((width, wide), BF16),
        ),
        in_specs=[HBM_SPEC] * 10,
        out_specs=(VMEM_SPEC,) * 3,
        scratch_shapes=[
            pltpu.SMEM(fwd_lengths.shape, jnp.int32),
            pltpu.SMEM(bwd_lengths.shape, jnp.int32),
            pltpu.VMEM((2, wide), BF16),
            pltpu.VMEM((rows, wide), BF16),
            pltpu.VMEM((rows, wide), BF16),
            pltpu.VMEM((rows, wide), BF16),
            pltpu.VMEM((wide, 3 * width), BF16),
            pltpu.VMEM((wide, 3 * width), BF16),
            pltpu.VMEM((width, wide), BF16),
            pltpu.VMEM((width, wide), BF16),
            pltpu.VMEM((rows + MOST, 3 * width), BF16),
            pltpu.VMEM((rows, 3 * width), BF16),
            pltpu.VMEM((rows, 3 * width), BF16),
            pltpu.VMEM((rows, width), BF16),
            pltpu.VMEM((2, rows, wide), BF16),
            pltpu.VMEM((2, share, wide), BF16),
            pltpu.VMEM((width, wide), BF16),
            pltpu.VMEM((2, 2, peers - 2, share, wide), BF16),
            pltpu.VMEM((2, 2, share, wide), BF16),
            pltpu.VMEM((2, 2, helper_count, wide), BF16),
            dma((16,)),
            dma((2, 2, peers - 1, pieces)),
            dma((2, 2, peers - 1, pieces)),
            dma((2, pieces)),
            dma((2, pieces)),
            dma((2,)),
            dma((2, 2, pieces)),
            dma((peers,)),
            dma((lenders, peers)),
            dma((lenders,)),
            dma,
        ],
        compiler_params=pltpu.CompilerParams(
            collective_id=0, has_side_effects=True, vmem_limit_bytes=VMEM_LIMIT
        ),
        cost_estimate=pl.CostEstimate(
            flops=28 * rows * wide * width,
            bytes_accessed=16 * wide * (rows + width),
            transcendentals=2 * rows * MOST,
        ),
        name="sections",
    )(
        fwd_lengths,
        bwd_lengths,
        norm_gains.reshape(2, wide),
        fwd_inputs,
        bwd_inputs,
        bwd_cotangent,
        query_weight,
        key_weight,
        value_weight,
        out_weight,
    )
    return results_of(moved, moved_grad, mirrored)


def solution(mesh):
    placed = (
        P("pipe", None, None),
        P("pipe", None, None),
        P("pipe", None, None),
        P("pipe", None),
        P("pipe", None),
        P(None, "pipe", None),
        P(None, "pipe", None, "tensor"),
        P(None, "pipe", None, "tensor"),
        P(None, "pipe", None, "tensor"),
        P(None, "pipe", "tensor", None),
    )
    return jax.shard_map(
        per_device,
        mesh=mesh,
        in_specs=placed,
        out_specs=(P("pipe", "tensor", None), P("pipe", "tensor", None), P("pipe", "tensor", None)),
        check_vma=False,
    )
```
